256 devices in a mesh: member: 32 (over z, x_hi, core), row: 4 (over y), col: 2 (over x_lo).
Axes of the slice: x: 4 (x_hi: 2, x_lo: 2; x = x_hi * 2 + x_lo), y: 4, z: 8, core: 2. Of those that a mesh axis runs over, the one named last changes fastest.
Arguments:
- pert: bfloat16 [32, 3, 2, 64, 1024], P('member', None, None, 'row', 'col'), may hold values from -6 to 6
- probes: bfloat16 [32, 3, 2, 64, 1024], P('member', None, None, 'row', 'col'), may hold values from -6 to 6
- diff_class: int32 [64, 1024], P('row', 'col'), may hold values from 0 to 7
- class_rate: float32 [8], replicated, may hold values from 0.03 to 0.24
Outputs:
- cov_probe: float32 [32, 3, 2, 64, 1024], P('member', None, None, 'row', 'col')
The draws below stay inside these ranges and needn't reach their ends.
All inputs are finite; a program needn't handle non-finite values.
Results may differ from the reference program's by a relative error of at most 0.0018.
Values may be sent and summed in bfloat16 or wider, within the bound.
No kernel may reach another device: no remote copies, remote signals or barrier semaphores. Data moves between devices by JAX's collectives and lax.ppermute only.
A program may use at most 128 MiB of HBM per device.

```python
import jax
import jax.numpy as jnp
from jax import lax

LEV = 2
VARS = 3
SWEEPS = 4
NCLASS = 8
MEMBERS = 32
PROBES = 32
NY = 64
NX = 1024


def plant(values, stream_key, least, largest):
    longest = values.shape.index(max(values.shape))
    spots = []
    for shift in (0, 1):
        where = [jax.random.randint(jax.random.fold_in(stream_key, axis), (), 0, length) for axis, length in enumerate(values.shape)]
        where[longest] = (where[longest] + shift) % values.shape[longest]
        spots.append(tuple(where))
    return values.at[spots[0]].set(least).at[spots[1]].set(largest)


def block_scale(stream_key, dims, split, low, largest):
    def one(axis_at, blocks):
        steps = jax.random.uniform(jax.random.fold_in(jax.random.fold_in(stream_key, 6), axis_at), (blocks,), jnp.float32, low / len(split), largest / len(split))
        return jnp.repeat(jnp.exp(steps), dims[axis_at] // blocks).reshape((-1,) + (1,) * (len(dims) - axis_at - 1))

    gain = one(*split[0])
    for cut in split[1:]:
        gain = gain * one(*cut)
    return gain


def centred(stream_key, shape, spread, limit, pieces=(), held_as=jnp.bfloat16):
    level = block_scale(stream_key, shape, pieces, -0.22, 0.18) if pieces else 1.0
    entries = jax.random.normal(stream_key, shape, jnp.float32) * spread * level
    return jnp.minimum(jnp.maximum(entries, -limit), limit).astype(held_as)


def setup_inputs(seed: int = 0) -> dict:
    key_list = jax.random.split(jax.random.key(seed), 5)
    return {
        "pert": centred(key_list[0], (MEMBERS, VARS, LEV, NY, NX), 1.0, 6.0, ((0, 32), (3, 4), (4, 2))),
        "probes": centred(key_list[1], (PROBES, VARS, LEV, NY, NX), 1.0, 6.0, ((0, 32), (3, 4), (4, 2))),
        "diff_class": plant(jax.random.randint(key_list[2], (NY, NX), 0, NCLASS), jax.random.fold_in(key_list[2], 1), 0, NCLASS - 1).astype(jnp.int32),
        "class_rate": jnp.clip(jax.random.uniform(key_list[3], (NCLASS,), jnp.float32, 0.03, 0.24), 0.03, 0.24),
    }


def class_rates(diff_class, class_rate):
    levels = jnp.arange(class_rate.shape[0], dtype=jnp.int32)
    picked = (diff_class[..., None] == levels).astype(jnp.float32)
    return jnp.sum(picked * class_rate.astype(jnp.float32), axis=-1)


def diffuse(field_now, cell_rate):
    widths = ((0, 0),) * (field_now.ndim - 2) + ((1, 1), (1, 1))
    padded = jnp.pad(field_now, widths)
    beside_all = padded[..., 2:, 1:-1] + padded[..., :-2, 1:-1] + padded[..., 1:-1, 2:] + padded[..., 1:-1, :-2]
    return field_now + cell_rate * (beside_all - 4.0 * field_now)


def reference(pert, probes, diff_class, class_rate):
    cell_rate = class_rates(diff_class, class_rate)
    probe_field = probes.astype(jnp.float32)

    def one_member(running, member):
        member_field = member.astype(jnp.float32)
        field_now = member_field[None] * probe_field
        for sweep_index in range(SWEEPS):
            field_now = diffuse(field_now, cell_rate)
        return running + member_field[None] * field_now, None

    running, unused = lax.scan(one_member, jnp.zeros(probe_field.shape, jnp.float32), pert)
    return running / (MEMBERS - 1)
```

```python
import jax
import jax.numpy as jnp
from jax import lax
from jax.experimental import pallas as pl
from jax.experimental.pallas import tpu as pltpu
from jax.sharding import PartitionSpec as P

SWEEPS = 4
VARS = 3
LEV = 2
ROWS = 16
COLS = 512
HALO = 4
STRIP = 32
WIN = STRIP + 2 * HALO
LANES = 128
F32 = jnp.float32
BF16 = jnp.bfloat16


def edge_kernel(col_ref, pert_ref, prob_ref, cls_ref, up_ref, dn_ref, side_ref, sup_ref, sdn_ref):
    last = col_ref[0] == 0
    for plane in range(VARS * LEV + 1):
        if plane < VARS * LEV:
            v, l = plane // LEV, plane % LEV
            a = pert_ref[0, v, l].astype(F32)
            b = prob_ref[0, v, l].astype(F32)
        else:
            a = (cls_ref[...] + 1).astype(F32)
            b = a
        up = jnp.concatenate([a[:HALO], b[:HALO]], axis=0)
        dn = jnp.concatenate([a[ROWS - HALO :], b[ROWS - HALO :]], axis=0)
        up_ref[plane] = up.astype(BF16)
        dn_ref[plane] = dn.astype(BF16)
        sup_ref[plane] = jnp.where(last, up[:, COLS - LANES :], up[:, :LANES]).astype(BF16)
        sdn_ref[plane] = jnp.where(last, dn[:, COLS - LANES :], dn[:, :LANES]).astype(BF16)
        side_ref[0, plane] = jnp.where(last, a[:, COLS - LANES :], a[:, :LANES]).astype(BF16)
        side_ref[1, plane] = jnp.where(last, b[:, COLS - LANES :], b[:, :LANES]).astype(BF16)


def pack_kernel(
    col_ref, pert_ref, prob_ref, cls_ref, below_ref, above_ref, side_ref, sbelow_ref, sabove_ref, out_ref, win_ref
):
    first = col_ref[0] == 0
    blocks = COLS // LANES
    lane = lax.broadcasted_iota(jnp.int32, (ROWS, LANES), 1)

    def block(kind, plane, at):
        inside = 0 <= at < blocks
        span = slice(at * LANES, (at + 1) * LANES)
        v, l = plane // LEV, plane % LEV
        if kind == 2:
            if inside:
                got = jnp.concatenate(
                    [below_ref[plane, :, span].astype(F32), above_ref[plane, :, span].astype(F32)], axis=0
                )
            else:
                got = jnp.concatenate([sbelow_ref[plane].astype(F32), sabove_ref[plane].astype(F32)], axis=0)
        elif not inside:
            got = side_ref[kind, plane].astype(F32)
        elif plane == VARS * LEV:
            got = (cls_ref[:, span] + 1).astype(F32)
        else:
            got = (pert_ref if kind == 0 else prob_ref)[0, v, l, :, span].astype(F32)
        if inside:
            return got
        return jnp.where(first if at == blocks else jnp.logical_not(first), got, 0.0)

    for at in range(-1, blocks + 1):
        span = slice((at + 1) * LANES, (at + 2) * LANES)
        win_ref[:ROWS, span] = block(0, VARS * LEV, at).astype(BF16)
        win_ref[ROWS:, span] = block(2, VARS * LEV, at).astype(BF16)

    for s in range(COLS // STRIP):
        start = s * STRIP - HALO
        at, off = start // LANES, start % LANES
        for l in range(LEV):
            for kind in range(3):
                acc = jnp.zeros((ROWS, LANES), F32)
                for v in range(VARS):
                    shift = (WIN * v - off) % LANES
                    got = block(kind, v * LEV + l, at)
                    got = pltpu.roll(got, shift, 1) if shift else got
                    if off + WIN > LANES:
                        more = block(kind, v * LEV + l, at + 1)
                        more = pltpu.roll(more, shift, 1) if shift else more
                        got = jnp.where(lane < WIN * v + LANES - off, got, more)
                    acc = jnp.where((lane >= WIN * v) & (lane < WIN * (v + 1)), got, acc)
                out_ref[s * LEV + l, kind * ROWS : (kind + 1) * ROWS] = acc.astype(BF16)


TOP = 8
TALL = TOP + ROWS + TOP
FORWARD = [
    (dy, dx)
    for dy in range(HALO + 1)
    for dx in range(-HALO, HALO + 1)
    if dy + abs(dx) <= HALO and (dy > 0 or dx >= 0)
]
EVERY = [(dy, dx) for dx in range(-HALO, HALO + 1) for dy in range(-HALO, HALO + 1) if abs(dy) + abs(dx) <= HALO]
AT = {d: i for i, d in enumerate(EVERY)}


def lanes_by(x, dx):
    return pltpu.roll(x, (-dx) % LANES, 1) if dx else x


def rows_by(x, dy):
    return pltpu.roll(x, (-dy) % x.shape[0], 0) if dy else x


def apply_kernel(strip_ref, rates_ref, got_ref, win_ref, out_ref, pert_ref, prob_ref, gram_ref, weight_ref):
    members = got_ref.shape[0]

    def spread(m, _):
        for ref, own, below, above in (
            (pert_ref, 0, 2 * ROWS, 2 * ROWS + 8),
            (prob_ref, ROWS, 2 * ROWS + 4, 2 * ROWS + 12),
        ):
            tile = got_ref[m].astype(F32)
            ref[m, 0:TOP] = jnp.zeros((TOP, LANES), F32)
            ref[m, TOP + ROWS : TALL] = jnp.zeros((TOP, LANES), F32)
            ref[m, TOP : TOP + ROWS] = tile[own : own + ROWS]
            ref[m, TOP + ROWS : TOP + ROWS + HALO] = tile[below : below + HALO]
            ref[m, TOP - HALO : TOP] = tile[above : above + HALO]
        return 0

    lax.fori_loop(0, members, spread, 0)

    wide = win_ref.shape[1]
    spot = lax.broadcasted_iota(jnp.int32, (wide, LANES), 0)
    lane = lax.broadcasted_iota(jnp.int32, (wide, LANES), 1)
    column = lane - jnp.where(lane >= WIN, WIN, 0) - jnp.where(lane >= 2 * WIN, WIN, 0)
    pick = (spot == LANES - HALO + STRIP * strip_ref[0] + column) & (lane < VARS * WIN)
    cls = jnp.dot(win_ref[...], pick.astype(F32).astype(BF16), preferred_element_type=F32)
    blank = jnp.zeros((TOP - HALO, LANES), F32)
    cls = jnp.concatenate(
        [blank, cls[ROWS + 8 : ROWS + 12], cls[:ROWS], cls[ROWS : ROWS + HALO], blank], axis=0
    )
    rate = jnp.zeros((TALL, LANES), F32)
    for k in range(rates_ref.shape[0]):
        rate = jnp.where(cls == float(k + 1), rates_ref[k], rate)

    steps = ((0, 1), (0, -1), (1, 0), (-1, 0))
    stay = 1.0 - 4.0 * rate
    coef = {(0, 0): stay}
    for e in steps:
        coef[e] = rate
    for sweep in range(1, SWEEPS):
        moved = {}
        for e in steps:
            for d, c in coef.items():
                to = (d[0] + e[0], d[1] + e[1])
                c = lanes_by(rows_by(c, e[0]), e[1])
                moved[to] = moved[to] + c if to in moved else c
        coef = {d: rate * moved[d] + (stay * coef[d] if d in coef else 0.0) for d in moved}
    scale = 1.0 / (members - 1)

    for b in range(3):
        row = TOP + 8 * b

        def products(m, acc):
            low = pert_ref[m, row : row + 8]
            high = [pert_ref[m, row - dy : row - dy + 8] for dy in range(HALO + 1)]
            near = {dx: lanes_by(low, dx) for dx in range(-HALO + 1, HALO + 1)}
            return tuple(a + high[dy] * near[dx] for a, (dy, dx) in zip(acc, FORWARD))

        acc = tuple(jnp.zeros((8, LANES), F32) for _ in FORWARD)
        acc = lax.fori_loop(0, members, products, acc, unroll=4)
        for i, a in enumerate(acc):
            gram_ref[i, 8 * b : 8 * b + 8] = a

    for i, (dy, dx) in enumerate(FORWARD):
        c = coef[(dy, dx)][TOP : TOP + ROWS] * scale
        weight_ref[AT[(dy, dx)]] = lanes_by(c * gram_ref[i, dy : dy + ROWS], -dx)
        if (dy, dx) != (0, 0):
            c = coef[(-dy, -dx)][TOP : TOP + ROWS] * scale
            weight_ref[AT[(-dy, -dx)]] = lanes_by(c, dx) * gram_ref[i, 0:ROWS]

    for b in range(2):

        def one_probe(p, _):
            rows = [prob_ref[p, TOP + 8 * b + dy : TOP + 8 * b + dy + 8] for dy in range(-HALO, HALO + 1)]
            total = None
            for dx in range(-HALO, HALO + 1):
                part = None
                for dy in range(-HALO + abs(dx), HALO - abs(dx) + 1):
                    term = weight_ref[AT[(dy, dx)], 8 * b : 8 * b + 8] * rows[dy + HALO]
                    part = term if part is None else part + term
                part = lanes_by(part, dx)
                total = part if total is None else total + part
            out_ref[p, 8 * b : 8 * b + 8] = total
            return 0

        lax.fori_loop(0, members, one_probe, 0, unroll=4)


def unpack_kernel(got_ref, out_ref):
    lane = lax.broadcasted_iota(jnp.int32, (ROWS, LANES), 1)
    per = LANES // STRIP
    for v in range(VARS):
        for l in range(LEV):
            for at in range(COLS // LANES):
                acc = None
                for q in range(per):
                    got = got_ref[(at * per + q) * LEV + l]
                    shift = (STRIP * q - WIN * v - HALO) % LANES
                    got = pltpu.roll(got, shift, 1) if shift else got
                    acc = got if acc is None else jnp.where(lane >= STRIP * q, got, acc)
                out_ref[0, v, l, :, at * LANES : (at + 1) * LANES] = acc


def body(pert, probes, diff_class, class_rate):
    members = lax.axis_size("member")
    n_row = lax.axis_size("row")
    col = lax.axis_index("col").astype(jnp.int32).reshape(1)
    strip = (lax.axis_index("member") // LEV).astype(jnp.int32).reshape(1)
    vmem = pl.BlockSpec(memory_space=pltpu.VMEM)
    smem = pl.BlockSpec(memory_space=pltpu.SMEM)
    planes = VARS * LEV + 1

    shape = jax.ShapeDtypeStruct
    up, dn, side, sup, sdn = pl.pallas_call(
        edge_kernel,
        in_specs=[smem, vmem, vmem, vmem],
        out_specs=[vmem] * 5,
        out_shape=[
            shape((planes, 2 * HALO, COLS), BF16),
            shape((planes, 2 * HALO, COLS), BF16),
            shape((2, planes, ROWS, LANES), BF16),
            shape((planes, 2 * HALO, LANES), BF16),
            shape((planes, 2 * HALO, LANES), BF16),
        ],
        name="edges",
    )(col, pert, probes, diff_class)

    below = lax.ppermute(up, "row", [(i + 1, i) for i in range(n_row - 1)])
    above = lax.ppermute(dn, "row", [(i, i + 1) for i in range(n_row - 1)])
    beside = lax.ppermute(side, "col", [(0, 1), (1, 0)])
    rc = ("row", "col")
    sbelow = lax.ppermute(sup, rc, [((i + 1) * 2 + c, i * 2 + 1 - c) for i in range(n_row - 1) for c in (0, 1)])
    sabove = lax.ppermute(sdn, rc, [(i * 2 + c, (i + 1) * 2 + 1 - c) for i in range(n_row - 1) for c in (0, 1)])

    chunks, window = pl.pallas_call(
        pack_kernel,
        in_specs=[smem] + [vmem] * 8,
        out_specs=[vmem] * 2,
        out_shape=[shape((members, 3 * ROWS, LANES), BF16), shape((2 * ROWS, COLS + 2 * LANES), BF16)],
        name="pack",
    )(col, pert, probes, diff_class, below, above, beside, sbelow, sabove)

    got = lax.all_to_all(chunks, "member", 0, 0, tiled=True)

    part = pl.pallas_call(
        apply_kernel,
        in_specs=[smem, smem, vmem, vmem],
        out_specs=vmem,
        out_shape=shape((members, ROWS, LANES), F32),
        scratch_shapes=[
            pltpu.VMEM((members, TALL, LANES), F32),
            pltpu.VMEM((members, TALL, LANES), F32),
            pltpu.VMEM((len(FORWARD), 24, LANES), F32),
            pltpu.VMEM((len(EVERY), ROWS, LANES), F32),
        ],
        name="apply",
    )(strip, class_rate, got, window)

    back = lax.all_to_all(part, "member", 0, 0, tiled=True)

    return pl.pallas_call(
        unpack_kernel,
        in_specs=[vmem],
        out_specs=vmem,
        out_shape=shape((1, VARS, LEV, ROWS, COLS), F32),
        name="unpack",
    )(back)


def solution(mesh):
    placed = (
        P("member", None, None, "row", "col"),
        P("member", None, None, "row", "col"),
        P("row", "col"),
        P(),
    )
    return jax.shard_map(
        body,
        mesh=mesh,
        in_specs=placed,
        out_specs=P("member", None, None, "row", "col"),
        check_vma=False,
    )
```

```python
import jax
import jax.numpy as jnp
from jax import lax
from jax.experimental import pallas as pl
from jax.experimental.pallas import tpu as pltpu
from jax.sharding import PartitionSpec as P

SWEEPS = 4
VARS = 3
LEV = 2
ROWS = 16
COLS = 512
HALO = 4
STRIP = 32
WIN = STRIP + 2 * HALO
LANES = 128
F32 = jnp.float32
BF16 = jnp.bfloat16


def side_kernel(col_ref, pert_ref, prob_ref, cls_ref, side_ref):
    last = col_ref[0] == 0
    for plane in range(2 * VARS * LEV + 1):
        if plane < 2 * VARS * LEV:
            ref = pert_ref if plane < VARS * LEV else prob_ref
            v, l = plane % (VARS * LEV) // LEV, plane % LEV
            head, tail = ref[0, v, l, :, :LANES].astype(F32), ref[0, v, l, :, COLS - LANES :].astype(F32)
        else:
            head, tail = (cls_ref[:, :LANES] + 1).astype(F32), (cls_ref[:, COLS - LANES :] + 1).astype(F32)
        side_ref[plane] = jnp.where(last, tail, head).astype(BF16)


def pack_kernel(col_ref, strip_ref, pert_ref, prob_ref, cls_ref, side_ref, out_ref, cls_out_ref, wide_ref):
    first = col_ref[0] == 0
    blocks = COLS // LANES
    lane = lax.broadcasted_iota(jnp.int32, (ROWS, LANES), 1)
    upper = lax.broadcasted_iota(jnp.int32, (8, LANES), 0) < HALO

    def block(plane, at):
        if 0 <= at < blocks:
            span = slice(at * LANES, (at + 1) * LANES)
            if plane == 2 * VARS * LEV:
                return (cls_ref[:, span] + 1).astype(F32)
            ref = pert_ref if plane < VARS * LEV else prob_ref
            return ref[0, plane % (VARS * LEV) // LEV, plane % LEV, :, span].astype(F32)
        got = side_ref[plane].astype(F32)
        return jnp.where(first if at == blocks else jnp.logical_not(first), got, 0.0)

    for s in range(COLS // STRIP):
        start = s * STRIP - HALO
        at, off = start // LANES, start % LANES
        for l in range(LEV):
            both = []
            for kind in range(2):
                acc = jnp.zeros((ROWS, LANES), F32)
                for v in range(VARS):
                    plane = (kind * VARS + v) * LEV + l
                    shift = (WIN * v - off) % LANES
                    got = block(plane, at)
                    got = pltpu.roll(got, shift, 1) if shift else got
                    if off + WIN > LANES:
                        more = block(plane, at + 1)
                        more = pltpu.roll(more, shift, 1) if shift else more
                        got = jnp.where(lane < WIN * v + LANES - off, got, more)
                    acc = jnp.where((lane >= WIN * v) & (lane < WIN * (v + 1)), got, acc)
                both.append(acc)
            a, b = both
            groups = [
                jnp.where(upper, a[:8], pltpu.roll(b[:8], HALO, 0)),
                jnp.where(upper, pltpu.roll(a[8:], HALO, 0), b[8:]),
                jnp.where(upper, pltpu.roll(a[:8], HALO, 0), b[:8]),
                jnp.where(upper, a[8:], pltpu.roll(b[8:], HALO, 0)),
            ]
            for pair in range(2):
                out_ref[s * LEV + l, pair * ROWS : (pair + 1) * ROWS] = jnp.concatenate(
                    groups[2 * pair : 2 * pair + 2], axis=0
                ).astype(BF16)

    for at in range(-1, blocks + 1):
        wide_ref[:, (at + 1) * LANES : (at + 2) * LANES] = block(2 * VARS * LEV, at).astype(BF16)
    wide = wide_ref.shape[1]
    spot = lax.broadcasted_iota(jnp.int32, (wide, LANES), 0)
    lane = lax.broadcasted_iota(jnp.int32, (wide, LANES), 1)
    column = lane - jnp.where(lane >= WIN, WIN, 0) - jnp.where(lane >= 2 * WIN, WIN, 0)
    pick = (spot == LANES - HALO + STRIP * strip_ref[0] + column) & (lane < VARS * WIN)
    cls_out_ref[...] = jnp.dot(wide_ref[...], pick.astype(F32).astype(BF16), preferred_element_type=F32)


def edge_kernel(got_ref, cls_ref, up_ref, dn_ref):
    members = got_ref.shape[0]
    up_ref[:members] = got_ref[:, :8]
    dn_ref[:members] = got_ref[:, 8:16]
    up_ref[members] = cls_ref[:8].astype(BF16)
    dn_ref[members] = pltpu.roll(cls_ref[8:], HALO, 0).astype(BF16)


TOP = 8
TALL = TOP + ROWS + TOP
FORWARD = [
    (dy, dx)
    for dy in range(HALO + 1)
    for dx in range(-HALO, HALO + 1)
    if dy + abs(dx) <= HALO and (dy > 0 or dx >= 0)
]
EVERY = [(dy, dx) for dx in range(-HALO, HALO + 1) for dy in range(-HALO, HALO + 1) if abs(dy) + abs(dx) <= HALO]
AT = {d: i for i, d in enumerate(EVERY)}


def lanes_by(x, dx):
    return pltpu.roll(x, (-dx) % LANES, 1) if dx else x


def rows_by(x, dy):
    return pltpu.roll(x, (-dy) % x.shape[0], 0) if dy else x


def apply_kernel(
    row_ref, rates_ref, got_ref, cls_ref, below_ref, above_ref, out_ref, pert_ref, prob_ref, gram_ref, weight_ref
):
    members = got_ref.shape[0]
    has_below = row_ref[0] != row_ref[1] - 1
    has_above = row_ref[0] != 0
    blank = jnp.zeros((HALO, LANES), F32)

    def spread(m, _):
        tile = got_ref[m].astype(F32)
        below = jnp.where(has_below, below_ref[m].astype(F32), 0.0)
        above = jnp.where(has_above, above_ref[m].astype(F32), 0.0)
        for ref, at in ((pert_ref, 0), (prob_ref, HALO)):
            ref[m, 0 : TOP - HALO] = blank
            ref[m, TOP - HALO : TOP] = above[at : at + HALO]
            for group, to in enumerate((0, 12, 4, 8)):
                ref[m, TOP + to : TOP + to + HALO] = tile[8 * group + at : 8 * group + at + HALO]
            ref[m, TOP + ROWS : TOP + ROWS + HALO] = below[at : at + HALO]
            ref[m, TOP + ROWS + HALO : TALL] = blank
        return 0

    lax.fori_loop(0, members, spread, 0, unroll=2)

    cls = jnp.concatenate(
        [
            blank,
            jnp.where(has_above, above_ref[members, :HALO].astype(F32), 0.0),
            cls_ref[...],
            jnp.where(has_below, below_ref[members, :HALO].astype(F32), 0.0),
            blank,
        ],
        axis=0,
    )
    rate = jnp.zeros((TALL, LANES), F32)
    for k in range(rates_ref.shape[0]):
        rate = jnp.where(cls == float(k + 1), rates_ref[k], rate)

    steps = ((0, 1), (0, -1), (1, 0), (-1, 0))
    stay = 1.0 - 4.0 * rate
    coef = {(0, 0): stay}
    for e in steps:
        coef[e] = rate
    for sweep in range(1, SWEEPS):
        moved = {}
        for e in steps:
            for d, c in coef.items():
                to = (d[0] + e[0], d[1] + e[1])
                c = lanes_by(rows_by(c, e[0]), e[1])
                moved[to] = moved[to] + c if to in moved else c
        coef = {d: rate * moved[d] + (stay * coef[d] if d in coef else 0.0) for d in moved}
    scale = 1.0 / (members - 1)

    for b in range(3):
        row = TOP + 8 * b

        def products(m, acc):
            low = pert_ref[m, row : row + 8]
            high = [pert_ref[m, row - dy : row - dy + 8] for dy in range(HALO + 1)]
            near = {dx: lanes_by(low, dx) for dx in range(-HALO + 1, HALO + 1)}
            return tuple(a + high[dy] * near[dx] for a, (dy, dx) in zip(acc, FORWARD))

        acc = tuple(jnp.zeros((8, LANES), F32) for _ in FORWARD)
        acc = lax.fori_loop(0, members, products, acc, unroll=4)
        for i, a in enumerate(acc):
            gram_ref[i, 8 * b : 8 * b + 8] = a

    for i, (dy, dx) in enumerate(FORWARD):
        c = coef[(dy, dx)][TOP : TOP + ROWS] * scale
        weight_ref[AT[(dy, dx)]] = lanes_by(c * gram_ref[i, dy : dy + ROWS], -dx)
        if (dy, dx) != (0, 0):
            c = coef[(-dy, -dx)][TOP : TOP + ROWS] * scale
            weight_ref[AT[(-dy, -dx)]] = lanes_by(c, dx) * gram_ref[i, 0:ROWS]

    for b in range(2):

        def one_probe(p, _):
            rows = [prob_ref[p, TOP + 8 * b + dy : TOP + 8 * b + dy + 8] for dy in range(-HALO, HALO + 1)]
            total = None
            for dx in range(-HALO, HALO + 1):
                part = None
                for dy in range(-HALO + abs(dx), HALO - abs(dx) + 1):
                    term = weight_ref[AT[(dy, dx)], 8 * b : 8 * b + 8] * rows[dy + HALO]
                    part = term if part is None else part + term
                part = lanes_by(part, dx)
                total = part if total is None else total + part
            out_ref[p, 8 * b : 8 * b + 8] = total
            return 0

        lax.fori_loop(0, members, one_probe, 0, unroll=4)


def unpack_kernel(got_ref, out_ref):
    lane = lax.broadcasted_iota(jnp.int32, (ROWS, LANES), 1)
    per = LANES // STRIP
    for v in range(VARS):
        for l in range(LEV):
            for at in range(COLS // LANES):
                acc = None
                for q in range(per):
                    got = got_ref[(at * per + q) * LEV + l]
                    shift = (STRIP * q - WIN * v - HALO) % LANES
                    got = pltpu.roll(got, shift, 1) if shift else got
                    acc = got if acc is None else jnp.where(lane >= STRIP * q, got, acc)
                out_ref[0, v, l, :, at * LANES : (at + 1) * LANES] = acc


def body(pert, probes, diff_class, class_rate):
    members = lax.axis_size("member")
    n_row = lax.axis_size("row")
    col = lax.axis_index("col").astype(jnp.int32).reshape(1)
    strip = (lax.axis_index("member") // LEV).astype(jnp.int32).reshape(1)
    vmem = pl.BlockSpec(memory_space=pltpu.VMEM)
    smem = pl.BlockSpec(memory_space=pltpu.SMEM)
    row = jnp.stack([lax.axis_index("row").astype(jnp.int32), jnp.int32(n_row)])
    planes = 2 * VARS * LEV + 1

    shape = pltpu.VMEM

    def near(x):
        return pltpu.with_memory_space_constraint(x, pltpu.VMEM)

    side = pl.pallas_call(
        side_kernel,
        in_specs=[smem, vmem, vmem, vmem],
        out_specs=vmem,
        out_shape=shape((planes, ROWS, LANES), BF16),
        name="side",
    )(col, pert, probes, diff_class)
    beside = lax.ppermute(side, "col", [(0, 1), (1, 0)])

    chunks, cls = pl.pallas_call(
        pack_kernel,
        in_specs=[smem] * 2 + [vmem] * 4,
        out_specs=[vmem] * 2,
        out_shape=[shape((members, 2 * ROWS, LANES), BF16), shape((ROWS, LANES), F32)],
        scratch_shapes=[pltpu.VMEM((ROWS, COLS + 2 * LANES), BF16)],
        name="pack",
    )(col, strip, pert, probes, diff_class, near(beside))

    got = lax.all_to_all(chunks, "member", 0, 0, tiled=True)

    edge = shape((members + 1, 8, LANES), BF16)
    up, dn = pl.pallas_call(
        edge_kernel,
        in_specs=[vmem] * 2,
        out_specs=[vmem] * 2,
        out_shape=[edge, edge],
        name="edges",
    )(near(got), near(cls))
    below = lax.ppermute(up, "row", [(i, (i - 1) % n_row) for i in range(n_row)])
    above = lax.ppermute(dn, "row", [(i, (i + 1) % n_row) for i in range(n_row)])

    part = pl.pallas_call(
        apply_kernel,
        in_specs=[smem, smem] + [vmem] * 4,
        out_specs=vmem,
        out_shape=shape((members, ROWS, LANES), F32),
        scratch_shapes=[
            pltpu.VMEM((members, TALL, LANES), F32),
            pltpu.VMEM((members, TALL, LANES), F32),
            pltpu.VMEM((len(FORWARD), 24, LANES), F32),
            pltpu.VMEM((len(EVERY), ROWS, LANES), F32),
        ],
        name="apply",
    )(row, class_rate, near(got), near(cls), near(below), near(above))

    back = lax.all_to_all(part, "member", 0, 0, tiled=True)

    return pl.pallas_call(
        unpack_kernel,
        in_specs=[vmem],
        out_specs=vmem,
        out_shape=jax.ShapeDtypeStruct((1, VARS, LEV, ROWS, COLS), F32),
        name="unpack",
    )(near(back))


def solution(mesh):
    placed = (
        P("member", None, None, "row", "col"),
        P("member", None, None, "row", "col"),
        P("row", "col"),
        P(),
    )
    return jax.shard_map(
        body,
        mesh=mesh,
        in_specs=placed,
        out_specs=P("member", None, None, "row", "col"),
        check_vma=False,
    )
```

```python
import functools

import jax
import jax.numpy as jnp
from jax import lax
from jax.experimental import pallas as pl
from jax.experimental.pallas import tpu as pltpu
from jax.sharding import PartitionSpec as P

SWEEPS = 4
VARS = 3
LEV = 2
ROWS = 16
COLS = 512
HALO = 4
STRIP = 32
WIN = STRIP + 2 * HALO
LANES = 128
F32 = jnp.float32
BF16 = jnp.bfloat16


def side_kernel(col_ref, pert_ref, prob_ref, cls_ref, side_ref):
    last = col_ref[0] == 0
    for plane in range(2 * VARS * LEV + 1):
        if plane < 2 * VARS * LEV:
            ref = pert_ref if plane < VARS * LEV else prob_ref
            v, l = plane % (VARS * LEV) // LEV, plane % LEV
            head, tail = ref[0, v, l, :, :LANES].astype(F32), ref[0, v, l, :, COLS - LANES :].astype(F32)
        else:
            head, tail = (cls_ref[:, :LANES] + 1).astype(F32), (cls_ref[:, COLS - LANES :] + 1).astype(F32)
        side_ref[plane] = jnp.where(last, tail, head).astype(BF16)


def shared(strips, planes_at, out):
    lane = lax.broadcasted_iota(jnp.int32, (ROWS, LANES), 1)
    upper = lax.broadcasted_iota(jnp.int32, (8, LANES), 0) < HALO
    for s in strips:
        start = s * STRIP - HALO
        at, off = start // LANES, start % LANES
        for l in range(LEV):
            both = []
            for kind in range(2):
                acc = jnp.zeros((ROWS, LANES), F32)
                for v in range(VARS):
                    plane = (kind * VARS + v) * LEV + l
                    shift = (WIN * v - off) % LANES
                    got = planes_at(plane, at)
                    got = pltpu.roll(got, shift, 1) if shift else got
                    if off + WIN > LANES:
                        more = planes_at(plane, at + 1)
                        more = pltpu.roll(more, shift, 1) if shift else more
                        got = jnp.where(lane < WIN * v + LANES - off, got, more)
                    acc = jnp.where((lane >= WIN * v) & (lane < WIN * (v + 1)), got, acc)
                both.append(acc)
            a, b = both
            groups = [
                jnp.where(upper, a[:8], pltpu.roll(b[:8], HALO, 0)),
                jnp.where(upper, pltpu.roll(a[8:], HALO, 0), b[8:]),
                jnp.where(upper, pltpu.roll(a[:8], HALO, 0), b[:8]),
                jnp.where(upper, a[8:], pltpu.roll(b[8:], HALO, 0)),
            ]
            for pair in range(2):
                rows = jnp.concatenate(groups[2 * pair : 2 * pair + 2], axis=0)
                out(s * LEV + l, pair, rows.astype(BF16))


def pack_kernel(pert_ref, prob_ref, out_ref):
    def block(plane, at):
        ref = pert_ref if plane < VARS * LEV else prob_ref
        span = slice(at * LANES, (at + 1) * LANES)
        return ref[0, plane % (VARS * LEV) // LEV, plane % LEV, :, span].astype(F32)

    def out(owner, pair, rows):
        out_ref[owner, pair * ROWS : (pair + 1) * ROWS] = rows

    shared(range(1, COLS // STRIP - 1), block, out)


def patch_kernel(col_ref, pert0_ref, prob0_ref, pert1_ref, prob1_ref, side_ref, all_ref, out_ref, new_ref, sems):
    first = col_ref[0] == 0
    blocks = COLS // LANES
    owners = LEV * COLS // STRIP

    def block(plane, at):
        if at in (-1, blocks):
            got = side_ref[plane].astype(F32)
            return jnp.where(first if at == blocks else jnp.logical_not(first), got, 0.0)
        refs = (pert0_ref, prob0_ref) if at == 0 else (pert1_ref, prob1_ref)
        ref = refs[0] if plane < VARS * LEV else refs[1]
        return ref[0, plane % (VARS * LEV) // LEV, plane % LEV].astype(F32)

    def out(owner, pair, rows):
        slot = owner if owner < LEV else owner - owners + 2 * LEV
        new_ref[slot, pair * ROWS : (pair + 1) * ROWS] = rows

    shared((0, COLS // STRIP - 1), block, out)
    head = pltpu.make_async_copy(new_ref.at[0:LEV], out_ref.at[0:LEV], sems.at[0])
    tail = pltpu.make_async_copy(new_ref.at[LEV : 2 * LEV], out_ref.at[owners - LEV : owners], sems.at[1])
    head.start()
    tail.start()
    head.wait()
    tail.wait()


def class_kernel(col_ref, strip_ref, cls_ref, side_ref, cls_out_ref, wide_ref):
    first = col_ref[0] == 0
    got = side_ref[2 * VARS * LEV].astype(F32)
    wide_ref[:, :LANES] = jnp.where(jnp.logical_not(first), got, 0.0).astype(BF16)
    wide_ref[:, LANES : LANES + COLS] = (cls_ref[...] + 1).astype(F32).astype(BF16)
    wide_ref[:, LANES + COLS :] = jnp.where(first, got, 0.0).astype(BF16)
    wide = wide_ref.shape[1]
    spot = lax.broadcasted_iota(jnp.int32, (wide, LANES), 0)
    lane = lax.broadcasted_iota(jnp.int32, (wide, LANES), 1)
    column = lane - jnp.where(lane >= WIN, WIN, 0) - jnp.where(lane >= 2 * WIN, WIN, 0)
    pick = (spot == LANES - HALO + STRIP * strip_ref[0] + column) & (lane < VARS * WIN)
    cls_out_ref[...] = jnp.dot(wide_ref[...], pick.astype(F32).astype(BF16), preferred_element_type=F32)


def edge_kernel(got_ref, cls_ref, up_ref, dn_ref):
    members = got_ref.shape[0]
    up_ref[:members] = got_ref[:, :8]
    dn_ref[:members] = got_ref[:, 8:16]
    up_ref[members] = cls_ref[:8].astype(BF16)
    dn_ref[members] = pltpu.roll(cls_ref[8:], HALO, 0).astype(BF16)


TOP = 8
TALL = TOP + ROWS + TOP
FORWARD = [
    (dy, dx)
    for dy in range(HALO + 1)
    for dx in range(-HALO, HALO + 1)
    if dy + abs(dx) <= HALO and (dy > 0 or dx >= 0)
]
EVERY = [(dy, dx) for dx in range(-HALO, HALO + 1) for dy in range(-HALO, HALO + 1) if abs(dy) + abs(dx) <= HALO]
AT = {d: i for i, d in enumerate(EVERY)}


def lanes_by(x, dx):
    return pltpu.roll(x, (-dx) % LANES, 1) if dx else x


def own_kernel(got_ref, gram_ref, pert_ref):
    members = got_ref.shape[0]
    blank = jnp.zeros((TOP, LANES), F32)

    def spread(m, _):
        tile = got_ref[m].astype(F32)
        pert_ref[m, 0:TOP] = blank
        for group, to in enumerate((0, 12, 4, 8)):
            pert_ref[m, TOP + to : TOP + to + HALO] = tile[8 * group : 8 * group + HALO]
        return 0

    lax.fori_loop(0, members, spread, 0, unroll=4)
    for b in range(2):
        row = TOP + 8 * b

        def products(m, acc):
            low = pert_ref[m, row : row + 8]
            high = [pert_ref[m, row - dy : row - dy + 8] for dy in range(HALO + 1)]
            near = {dx: lanes_by(low, dx) for dx in range(-HALO + 1, HALO + 1)}
            return tuple(a + high[dy] * near[dx] for a, (dy, dx) in zip(acc, FORWARD))

        acc = tuple(jnp.zeros((8, LANES), F32) for _ in FORWARD)
        acc = lax.fori_loop(0, members, products, acc, unroll=4)
        for i, a in enumerate(acc):
            gram_ref[i, 8 * b : 8 * b + 8] = a


def apply_kernel(
    n_row, row_ref, rates_ref, got_ref, cls_ref, below_ref, above_ref, own_ref, out_ref,
    prob_ref, gram_ref, weight_ref, rate_ref,
):
    members = got_ref.shape[0]
    has_below = row_ref[0] != n_row - 1
    has_above = row_ref[0] != 0
    blank = jnp.zeros((HALO, LANES), F32)
    sub = lax.broadcasted_iota(jnp.int32, (8, LANES), 0)
    lane = lax.broadcasted_iota(jnp.int32, (8, LANES), 1)
    upper = sub < HALO
    crossing = [d for d in FORWARD if d[0] > 0]

    def spread(m, acc):
        tile = got_ref[m].astype(F32)
        below = jnp.where(has_below, below_ref[m].astype(F32), 0.0)
        above = jnp.where(has_above, above_ref[m].astype(F32), 0.0)
        prob_ref[m, 0 : TOP - HALO] = blank
        prob_ref[m, TOP - HALO : TOP] = above[HALO:]
        for group, to in enumerate((0, 12, 4, 8)):
            prob_ref[m, TOP + to : TOP + to + HALO] = tile[8 * group + HALO : 8 * group + 8]
        prob_ref[m, TOP + ROWS : TOP + ROWS + HALO] = below[HALO:]
        prob_ref[m, TOP + ROWS + HALO : TALL] = blank
        low = jnp.where(upper, tile[0:8], pltpu.roll(below, HALO, 0))
        high = jnp.where(upper, above, pltpu.roll(tile[8:16], HALO, 0))
        high = {dy: pltpu.roll(high, HALO + dy, 0) if dy < HALO else high for dy in range(1, HALO + 1)}
        near = {dx: lanes_by(low, dx) for dx in range(-HALO + 1, HALO)}
        return tuple(a + high[dy] * near[dx] for a, (dy, dx) in zip(acc, crossing))

    acc = tuple(jnp.zeros((8, LANES), F32) for _ in crossing)
    acc = dict(zip(crossing, lax.fori_loop(0, members, spread, acc, unroll=4)))
    for i, d in enumerate(FORWARD):
        gram_ref[i, 8:16] = own_ref[i, 8:16]
        if d in acc:
            gram_ref[i, 0:8] = own_ref[i, 0:8] + jnp.where(sub < d[0], acc[d], 0.0)
            gram_ref[i, 16:24] = pltpu.roll(acc[d], HALO, 0)
        else:
            gram_ref[i, 0:8] = own_ref[i, 0:8]

    cls = jnp.concatenate(
        [
            blank,
            jnp.where(has_above, above_ref[members, :HALO].astype(F32), 0.0),
            cls_ref[...],
            jnp.where(has_below, below_ref[members, :HALO].astype(F32), 0.0),
            blank,
        ],
        axis=0,
    )
    rate = jnp.zeros((TALL, LANES), F32)
    for k in range(rates_ref.shape[0]):
        rate = jnp.where(cls == float(k + 1), rates_ref[k], rate)
    rate_ref[...] = rate

    steps = ((0, 1), (0, -1), (1, 0), (-1, 0))
    at = {
        (dy, dx): lanes_by(rate_ref[TOP + dy : TOP + dy + ROWS], dx)
        for dy, dx in EVERY
        if abs(dy) + abs(dx) < HALO
    }
    coef = {(0, 0): 1.0 - 4.0 * at[(0, 0)]}
    for e in steps:
        coef[e] = at[(0, 0)]
    for sweep in range(1, SWEEPS):
        flow = {d: c * at[d] for d, c in coef.items()}
        to = {(d[0] + e[0], d[1] + e[1]) for d in flow for e in steps}
        new = {}
        for d in EVERY:
            if d not in to:
                continue
            terms = [flow[(d[0] - e[0], d[1] - e[1])] for e in steps if (d[0] - e[0], d[1] - e[1]) in flow]
            if d in coef:
                terms.append(coef[d] - 4.0 * flow[d])
            total = terms[0]
            for t in terms[1:]:
                total = total + t
            new[d] = total
        coef = new
    scale = 1.0 / (members - 1)

    for i, (dy, dx) in enumerate(FORWARD):
        weight_ref[AT[(dy, dx)]] = lanes_by(coef[(dy, dx)] * scale * gram_ref[i, dy : dy + ROWS], -dx)
        if (dy, dx) != (0, 0):
            weight_ref[AT[(-dy, -dx)]] = lanes_by(coef[(-dy, -dx)] * scale, dx) * gram_ref[i, 0:ROWS]

    def one_probe(p, _):
        both = []
        for b in range(2):
            rows = [prob_ref[p, TOP + 8 * b + dy : TOP + 8 * b + dy + 8] for dy in range(-HALO, HALO + 1)]
            total = None
            for dx in range(-HALO, HALO + 1):
                part = None
                for dy in range(-HALO + abs(dx), HALO - abs(dx) + 1):
                    term = weight_ref[AT[(dy, dx)], 8 * b : 8 * b + 8] * rows[dy + HALO]
                    part = term if part is None else part + term
                part = lanes_by(part, dx)
                total = part if total is None else total + part
            both.append(total)
        a, b = both
        first = jnp.where(lane < STRIP, lanes_by(a, HALO), lanes_by(a, HALO + 8))
        first = jnp.where(lane < 2 * STRIP, first, lanes_by(a, HALO + 16))
        first = jnp.where(lane < 3 * STRIP, first, lanes_by(b, HALO - 3 * STRIP))
        rest = jnp.where(lane < STRIP, lanes_by(b, WIN + HALO), lanes_by(b, 2 * WIN + HALO - STRIP))
        rest = jnp.where(lane < 2 * STRIP, rest, pltpu.roll(lanes_by(rest, 2 * STRIP), HALO, 0))
        out_ref[p, 0] = first[:HALO]
        out_ref[p, 1] = first[HALO:]
        out_ref[p, 2] = rest[:HALO]
        return 0

    lax.fori_loop(0, members, one_probe, 0, unroll=4)


def unpack_kernel(got_ref, out_ref):
    lane = lax.broadcasted_iota(jnp.int32, (ROWS, LANES), 1)
    per = LANES // STRIP

    def moved(x, shift):
        shift %= LANES
        return pltpu.roll(x, shift, 1) if shift else x

    for l in range(LEV):
        for at in range(COLS // LANES):
            acc = [None] * VARS
            for q in range(per):
                got = got_ref[(at * per + q) * LEV + l]
                top = jnp.concatenate([got[0], got[1]], axis=0)
                low = jnp.concatenate([got[2], moved(got[2], 2 * STRIP)], axis=0)
                for v in range(VARS):
                    under = moved(top, STRIP * (q - VARS)) if v == 0 else moved(low, STRIP * (q - v + 1))
                    piece = jnp.concatenate([moved(top, STRIP * (q - v)), under], axis=0)
                    acc[v] = piece if acc[v] is None else jnp.where(lane >= STRIP * q, piece, acc[v])
            for v in range(VARS):
                out_ref[0, v, l, :, at * LANES : (at + 1) * LANES] = acc[v]


def body(pert, probes, diff_class, class_rate):
    members = lax.axis_size("member")
    n_row = lax.axis_size("row")
    col = lax.axis_index("col").astype(jnp.int32).reshape(1)
    strip = (lax.axis_index("member") // LEV).astype(jnp.int32).reshape(1)
    vmem = pl.BlockSpec(memory_space=pltpu.VMEM)
    smem = pl.BlockSpec(memory_space=pltpu.SMEM)
    row = lax.axis_index("row").astype(jnp.int32).reshape(1)
    planes = 2 * VARS * LEV + 1

    shape = pltpu.VMEM

    def near(x):
        return pltpu.with_memory_space_constraint(x, pltpu.VMEM)

    side = pl.pallas_call(
        side_kernel,
        in_specs=[smem, vmem, vmem, vmem],
        out_specs=vmem,
        out_shape=shape((planes, ROWS, LANES), BF16),
        name="side",
    )(col, pert, probes, diff_class)
    beside = lax.ppermute(side, "col", [(0, 1), (1, 0)])

    chunk = jax.ShapeDtypeStruct((members, 2 * ROWS, LANES), BF16)
    inner = pl.pallas_call(pack_kernel, in_specs=[vmem] * 2, out_specs=vmem, out_shape=chunk, name="pack")(pert, probes)
    ends = [
        pl.BlockSpec((1, VARS, LEV, ROWS, LANES), lambda i: (0, 0, 0, 0, 0)),
        pl.BlockSpec((1, VARS, LEV, ROWS, LANES), lambda i: (0, 0, 0, 0, COLS // LANES - 1)),
    ]
    chunks = pl.pallas_call(
        patch_kernel,
        grid=(1,),
        in_specs=[smem, ends[0], ends[0], ends[1], ends[1], vmem, pl.BlockSpec(memory_space=pl.ANY)],
        out_specs=pl.BlockSpec(memory_space=pl.ANY),
        out_shape=chunk,
        scratch_shapes=[pltpu.VMEM((2 * LEV, 2 * ROWS, LANES), BF16), pltpu.SemaphoreType.DMA((2,))],
        input_output_aliases={6: 0},
        name="patch",
    )(col, pert, probes, pert, probes, near(beside), inner)
    cls = pl.pallas_call(
        class_kernel,
        in_specs=[smem] * 2 + [vmem] * 2,
        out_specs=vmem,
        out_shape=shape((ROWS, LANES), F32),
        scratch_shapes=[pltpu.VMEM((ROWS, COLS + 2 * LANES), BF16)],
        name="classes",
    )(col, strip, diff_class, near(beside))

    got = lax.all_to_all(chunks, "member", 0, 0, tiled=True)

    edge = shape((members + 1, 8, LANES), BF16)
    up, dn = pl.pallas_call(
        edge_kernel,
        in_specs=[vmem] * 2,
        out_specs=[vmem] * 2,
        out_shape=[edge, edge],
        name="edges",
    )(near(got), near(cls))
    below = lax.ppermute(up, "row", [(i, (i - 1) % n_row) for i in range(n_row)])
    above = lax.ppermute(dn, "row", [(i, (i + 1) % n_row) for i in range(n_row)])

    own = pl.pallas_call(
        own_kernel,
        in_specs=[vmem],
        out_specs=vmem,
        out_shape=shape((len(FORWARD), ROWS, LANES), F32),
        scratch_shapes=[pltpu.VMEM((members, TOP + ROWS, LANES), F32)],
        name="own",
    )(near(got))

    part = pl.pallas_call(
        functools.partial(apply_kernel, n_row),
        in_specs=[smem, smem] + [vmem] * 5,
        out_specs=vmem,
        out_shape=shape((members, VARS, HALO, LANES), F32),
        scratch_shapes=[
            pltpu.VMEM((members, TALL, LANES), F32),
            pltpu.VMEM((len(FORWARD), 24, LANES), F32),
            pltpu.VMEM((len(EVERY), ROWS, LANES), F32),
            pltpu.VMEM((TALL, LANES), F32),
        ],
        name="apply",
    )(row, class_rate, near(got), near(cls), near(below), near(above), near(own))

    back = lax.all_to_all(part, "member", 0, 0, tiled=True)

    return pl.pallas_call(
        unpack_kernel,
        in_specs=[vmem],
        out_specs=vmem,
        out_shape=jax.ShapeDtypeStruct((1, VARS, LEV, ROWS, COLS), F32),
        name="unpack",
    )(near(back))


def solution(mesh):
    placed = (
        P("member", None, None, "row", "col"),
        P("member", None, None, "row", "col"),
        P("row", "col"),
        P(),
    )
    return jax.shard_map(
        body,
        mesh=mesh,
        in_specs=placed,
        out_specs=P("member", None, None, "row", "col"),
        check_vma=False,
    )
```

```python
import functools

import jax
import jax.numpy as jnp
from jax import lax
from jax.experimental import pallas as pl
from jax.experimental.pallas import tpu as pltpu
from jax.sharding import PartitionSpec as P

SWEEPS = 4
VARS = 3
LEV = 2
ROWS = 16
COLS = 512
HALO = 4
STRIP = 32
WIN = STRIP + 2 * HALO
LANES = 128
F32 = jnp.float32
BF16 = jnp.bfloat16


def grouped(a, b):
    upper = lax.broadcasted_iota(jnp.int32, (8, LANES), 0) < HALO
    groups = [
        jnp.where(upper, a[:8], pltpu.roll(b[:8], HALO, 0)),
        jnp.where(upper, pltpu.roll(a[8:], HALO, 0), b[8:]),
        jnp.where(upper, pltpu.roll(a[:8], HALO, 0), b[:8]),
        jnp.where(upper, a[8:], pltpu.roll(b[8:], HALO, 0)),
    ]
    return jnp.concatenate(groups, axis=0).astype(BF16)


def side_kernel(pert_ref, prob_ref, cls_ref, side_ref):
    last = lax.axis_index("col") == 0
    lane = lax.broadcasted_iota(jnp.int32, (ROWS, LANES), 1)
    use = [
        (lane >= WIN * v + jnp.where(last, 0, WIN - HALO)) & (lane < WIN * v + jnp.where(last, HALO, WIN))
        for v in range(VARS)
    ]

    def placed(blocks):
        acc = jnp.zeros((ROWS, LANES), F32)
        for v, (head, tail) in enumerate(blocks):
            tail = pltpu.roll(tail, (WIN * v + HALO) % LANES, 1)
            head = pltpu.roll(head, (WIN * v + WIN - HALO) % LANES, 1)
            acc = jnp.where(use[v], jnp.where(last, tail, head), acc)
        return acc

    def ends(ref, v, l):
        return ref[0, v, l, :, :LANES].astype(F32), ref[0, v, l, :, COLS - LANES :].astype(F32)

    for l in range(LEV):
        a, b = (placed([ends(ref, v, l) for v in range(VARS)]) for ref in (pert_ref, prob_ref))
        side_ref[l * 2 * ROWS : (l + 1) * 2 * ROWS] = grouped(a, b)
    cls = ((cls_ref[:, :LANES] + 1).astype(F32), (cls_ref[:, COLS - LANES :] + 1).astype(F32))
    side_ref[LEV * 2 * ROWS :] = placed([cls] * VARS).astype(BF16)


def pack_kernel(pert_ref, prob_ref, cls_ref, out_ref, cls_out_ref, wide_ref):
    lane = lax.broadcasted_iota(jnp.int32, (ROWS, LANES), 1)
    blocks = COLS // LANES

    def block(ref, v, l, at, shift):
        got = ref[0, v, l, :, at * LANES : (at + 1) * LANES].astype(F32)
        return pltpu.roll(got, shift, 1) if shift else got

    for s in range(COLS // STRIP):
        start = s * STRIP - HALO
        at, off = start // LANES, start % LANES
        for l in range(LEV):
            both = []
            for ref in (pert_ref, prob_ref):
                acc = jnp.zeros((ROWS, LANES), F32)
                for v in range(VARS):
                    shift = (WIN * v - off) % LANES
                    low, high = WIN * v, WIN * (v + 1)
                    split = low + LANES - off
                    if at >= 0:
                        use = (lane >= low) & (lane < min(high, split))
                        acc = jnp.where(use, block(ref, v, l, at, shift), acc)
                    if split < high and at + 1 < blocks:
                        use = (lane >= split) & (lane < high)
                        acc = jnp.where(use, block(ref, v, l, at + 1, shift), acc)
                both.append(acc)
            out_ref[s * LEV + l] = grouped(*both)

    zero = jnp.zeros((ROWS, LANES), BF16)
    wide_ref[:, :LANES] = zero
    wide_ref[:, LANES : LANES + COLS] = (cls_ref[...] + 1).astype(F32).astype(BF16)
    wide_ref[:, LANES + COLS :] = zero
    strip = lax.axis_index("member") // LEV
    wide = wide_ref.shape[1]
    spot = lax.broadcasted_iota(jnp.int32, (wide, LANES), 0)
    lane = lax.broadcasted_iota(jnp.int32, (wide, LANES), 1)
    column = lane - jnp.where(lane >= WIN, WIN, 0) - jnp.where(lane >= 2 * WIN, WIN, 0)
    pick = (spot == LANES - HALO + STRIP * strip + column) & (lane < VARS * WIN)
    cls_out_ref[...] = jnp.dot(wide_ref[...], pick.astype(F32).astype(BF16), preferred_element_type=F32)


def patch_kernel(side_ref, inner_ref, cls_ref, out_ref, cls_out_ref):
    first = lax.axis_index("col") == 0
    strip = lax.axis_index("member") // LEV
    end = COLS // STRIP - 1
    for l in range(LEV):
        side = side_ref[l * 2 * ROWS : (l + 1) * 2 * ROWS].astype(F32)
        for s, here in ((0, jnp.logical_not(first)), (end, first)):
            at = s * LEV + l
            out_ref[at] = (inner_ref[at].astype(F32) + jnp.where(here, side, 0.0)).astype(BF16)
    mine = strip == jnp.where(first, end, 0)
    cls_out_ref[...] = cls_ref[...] + jnp.where(mine, side_ref[LEV * 2 * ROWS :].astype(F32), 0.0)


def edge_kernel(got_ref, cls_ref, up_ref, dn_ref):
    members = got_ref.shape[0]
    up_ref[:members] = got_ref[:, :8]
    dn_ref[:members] = got_ref[:, 8:16]
    up_ref[members] = cls_ref[:8].astype(BF16)
    dn_ref[members] = pltpu.roll(cls_ref[8:], HALO, 0).astype(BF16)


TOP = 8
TALL = TOP + ROWS + TOP
FORWARD = [
    (dy, dx)
    for dy in range(HALO + 1)
    for dx in range(-HALO, HALO + 1)
    if dy + abs(dx) <= HALO and (dy > 0 or dx >= 0)
]
EVERY = [(dy, dx) for dx in range(-HALO, HALO + 1) for dy in range(-HALO, HALO + 1) if abs(dy) + abs(dx) <= HALO]
AT = {d: i for i, d in enumerate(EVERY)}


def lanes_by(x, dx):
    return pltpu.roll(x, (-dx) % LANES, 1) if dx else x


def own_kernel(got_ref, gram_ref, prob_ref, pert_ref):
    members = got_ref.shape[0]
    blank = jnp.zeros((TOP, LANES), F32)

    def spread(m, _):
        tile = got_ref[m].astype(F32)
        pert_ref[m, 0:TOP] = blank
        for group, to in enumerate((0, 12, 4, 8)):
            pert_ref[m, TOP + to : TOP + to + HALO] = tile[8 * group : 8 * group + HALO]
            prob_ref[m, TOP + to : TOP + to + HALO] = tile[8 * group + HALO : 8 * group + 8]
        return 0

    lax.fori_loop(0, members, spread, 0, unroll=4)
    for b in range(2):
        row = TOP + 8 * b

        def products(m, acc):
            low = pert_ref[m, row : row + 8]
            high = [pert_ref[m, row - dy : row - dy + 8] for dy in range(HALO + 1)]
            near = {dx: lanes_by(low, dx) for dx in range(-HALO + 1, HALO + 1)}
            return tuple(a + high[dy] * near[dx] for a, (dy, dx) in zip(acc, FORWARD))

        acc = tuple(jnp.zeros((8, LANES), F32) for _ in FORWARD)
        acc = lax.fori_loop(0, members, products, acc, unroll=4)
        for i, a in enumerate(acc):
            gram_ref[i, 8 * b : 8 * b + 8] = a


def apply_kernel(
    n_row, rates_ref, got_ref, cls_ref, below_ref, above_ref, own_ref, part_ref, out_ref,
    prob_ref, gram_ref, weight_ref, rate_ref,
):
    members = got_ref.shape[0]
    has_below = lax.axis_index("row") != n_row - 1
    has_above = lax.axis_index("row") != 0
    blank = jnp.zeros((HALO, LANES), F32)
    sub = lax.broadcasted_iota(jnp.int32, (8, LANES), 0)
    lane = lax.broadcasted_iota(jnp.int32, (8, LANES), 1)
    upper = sub < HALO
    crossing = [d for d in FORWARD if d[0] > 0]

    def spread(m, acc):
        tile = got_ref[m, :ROWS].astype(F32)
        below = jnp.where(has_below, below_ref[m].astype(F32), 0.0)
        above = jnp.where(has_above, above_ref[m].astype(F32), 0.0)
        prob_ref[m, TOP - HALO : TOP] = above[HALO:]
        prob_ref[m, TOP + ROWS : TOP + ROWS + HALO] = below[HALO:]
        low = jnp.where(upper, tile[0:8], pltpu.roll(below, HALO, 0))
        high = jnp.where(upper, above, pltpu.roll(tile[8:16], HALO, 0))
        high = {dy: pltpu.roll(high, HALO + dy, 0) if dy < HALO else high for dy in range(1, HALO + 1)}
        near = {dx: lanes_by(low, dx) for dx in range(-HALO + 1, HALO)}
        return tuple(a + high[dy] * near[dx] for a, (dy, dx) in zip(acc, crossing))

    acc = tuple(jnp.zeros((8, LANES), F32) for _ in crossing)
    acc = dict(zip(crossing, lax.fori_loop(0, members, spread, acc, unroll=4)))
    for i, d in enumerate(FORWARD):
        gram_ref[i, 8:16] = own_ref[i, 8:16]
        if d in acc:
            gram_ref[i, 0:8] = own_ref[i, 0:8] + jnp.where(sub < d[0], acc[d], 0.0)
            gram_ref[i, 16:24] = pltpu.roll(acc[d], HALO, 0)
        else:
            gram_ref[i, 0:8] = own_ref[i, 0:8]

    cls = jnp.concatenate(
        [
            blank,
            jnp.where(has_above, above_ref[members, :HALO].astype(F32), 0.0),
            cls_ref[...],
            jnp.where(has_below, below_ref[members, :HALO].astype(F32), 0.0),
            blank,
        ],
        axis=0,
    )
    rate = jnp.zeros((TALL, LANES), F32)
    for k in range(rates_ref.shape[0]):
        rate = jnp.where(cls == float(k + 1), rates_ref[k], rate)
    rate_ref[...] = rate

    steps = ((0, 1), (0, -1), (1, 0), (-1, 0))
    at = {
        (dy, dx): lanes_by(rate_ref[TOP + dy : TOP + dy + ROWS], dx)
        for dy, dx in EVERY
        if abs(dy) + abs(dx) < HALO
    }
    coef = {(0, 0): 1.0 - 4.0 * at[(0, 0)]}
    for e in steps:
        coef[e] = at[(0, 0)]
    for sweep in range(1, SWEEPS):
        flow = {d: c * at[d] for d, c in coef.items()}
        to = {(d[0] + e[0], d[1] + e[1]) for d in flow for e in steps}
        new = {}
        for d in EVERY:
            if d not in to:
                continue
            terms = [flow[(d[0] - e[0], d[1] - e[1])] for e in steps if (d[0] - e[0], d[1] - e[1]) in flow]
            if d in coef:
                terms.append(coef[d] - 4.0 * flow[d])
            total = terms[0]
            for t in terms[1:]:
                total = total + t
            new[d] = total
        coef = new
    scale = 1.0 / (members - 1)

    for i, (dy, dx) in enumerate(FORWARD):
        weight_ref[AT[(dy, dx)]] = lanes_by(coef[(dy, dx)] * scale * gram_ref[i, dy : dy + ROWS], -dx)
        if (dy, dx) != (0, 0):
            weight_ref[AT[(-dy, -dx)]] = lanes_by(coef[(-dy, -dx)] * scale, dx) * gram_ref[i, 0:ROWS]

    def probe_pair(i, _):
        pair = (2 * i, 2 * i + 1)
        both = [[], []]
        for b in range(2):
            rows = [
                [prob_ref[p, TOP + 8 * b + dy : TOP + 8 * b + dy + 8] for dy in range(-HALO, HALO + 1)] for p in pair
            ]
            total = [None, None]
            for dx in range(-HALO, HALO + 1):
                part = [None, None]
                for dy in range(-HALO + abs(dx), HALO - abs(dx) + 1):
                    weight = weight_ref[AT[(dy, dx)], 8 * b : 8 * b + 8]
                    for j in range(2):
                        term = weight * rows[j][dy + HALO]
                        part[j] = term if part[j] is None else part[j] + term
                for j in range(2):
                    moved = lanes_by(part[j], dx)
                    total[j] = moved if total[j] is None else total[j] + moved
            for j in range(2):
                both[j].append(total[j])
        for p, (a, b) in zip(pair, both):
            first = jnp.where(lane < STRIP, lanes_by(a, HALO), lanes_by(a, HALO + 8))
            first = jnp.where(lane < 2 * STRIP, first, lanes_by(a, HALO + 16))
            first = jnp.where(lane < 3 * STRIP, first, lanes_by(b, HALO - 3 * STRIP))
            rest = jnp.where(lane < STRIP, lanes_by(b, WIN + HALO), lanes_by(b, 2 * WIN + HALO - STRIP))
            rest = jnp.where(lane < 2 * STRIP, rest, pltpu.roll(lanes_by(rest, 2 * STRIP), HALO, 0))
            out_ref[p, 0] = first[:HALO]
            out_ref[p, 1] = first[HALO:]
            out_ref[p, 2] = rest[:HALO]
        return 0

    lax.fori_loop(0, members // 2, probe_pair, 0, unroll=2)


def unpack_kernel(got_ref, out_ref):
    lane = lax.broadcasted_iota(jnp.int32, (ROWS, LANES), 1)
    per = LANES // STRIP

    def moved(x, shift):
        shift %= LANES
        return pltpu.roll(x, shift, 1) if shift else x

    for l in range(LEV):
        for at in range(COLS // LANES):
            acc = [None] * VARS
            for q in range(per):
                got = got_ref[(at * per + q) * LEV + l]
                top = jnp.concatenate([got[0], got[1]], axis=0)
                low = jnp.concatenate([got[2], moved(got[2], 2 * STRIP)], axis=0)
                for v in range(VARS):
                    under = moved(top, STRIP * (q - VARS)) if v == 0 else moved(low, STRIP * (q - v + 1))
                    piece = jnp.concatenate([moved(top, STRIP * (q - v)), under], axis=0)
                    acc[v] = piece if acc[v] is None else jnp.where(lane >= STRIP * q, piece, acc[v])
            for v in range(VARS):
                out_ref[0, v, l, :, at * LANES : (at + 1) * LANES] = acc[v]


def body(pert, probes, diff_class, class_rate):
    members = lax.axis_size("member")
    n_row = lax.axis_size("row")
    vmem = pl.BlockSpec(memory_space=pltpu.VMEM)
    smem = pl.BlockSpec(memory_space=pltpu.SMEM)
    shape = pltpu.VMEM

    def near(x):
        return pltpu.with_memory_space_constraint(x, pltpu.VMEM)

    side = pl.pallas_call(
        side_kernel,
        in_specs=[vmem] * 3,
        out_specs=vmem,
        out_shape=shape(((2 * LEV + 1) * ROWS, LANES), BF16),
        name="side",
    )(pert, probes, diff_class)
    beside = lax.ppermute(side, "col", [(0, 1), (1, 0)])

    chunk, classes = shape((members, 2 * ROWS, LANES), BF16), shape((ROWS, LANES), F32)
    inner, cls = pl.pallas_call(
        pack_kernel,
        in_specs=[vmem] * 3,
        out_specs=[vmem] * 2,
        out_shape=[chunk, classes],
        scratch_shapes=[pltpu.VMEM((ROWS, COLS + 2 * LANES), BF16)],
        name="pack",
    )(pert, probes, diff_class)
    chunks, cls = pl.pallas_call(
        patch_kernel,
        in_specs=[vmem] * 3,
        out_specs=[vmem] * 2,
        out_shape=[chunk, classes],
        input_output_aliases={1: 0},
        name="patch",
    )(near(beside), near(inner), near(cls))

    got = lax.all_to_all(chunks, "member", 0, 0, tiled=True)

    edge = shape((members + 1, 8, LANES), BF16)
    up, dn = pl.pallas_call(
        edge_kernel,
        in_specs=[vmem] * 2,
        out_specs=[vmem] * 2,
        out_shape=[edge, edge],
        name="edges",
    )(near(got), near(cls))
    below = lax.ppermute(up, "row", [(i, (i - 1) % n_row) for i in range(n_row)])
    above = lax.ppermute(dn, "row", [(i, (i + 1) % n_row) for i in range(n_row)])

    tall = shape((members, TALL, LANES), F32)
    own, spread = pl.pallas_call(
        own_kernel,
        in_specs=[vmem],
        out_specs=[vmem] * 2,
        out_shape=[shape((len(FORWARD), ROWS, LANES), F32), tall],
        scratch_shapes=[pltpu.VMEM((members, TOP + ROWS, LANES), F32)],
        name="own",
    )(near(got))

    part, spread = pl.pallas_call(
        functools.partial(apply_kernel, n_row),
        in_specs=[smem] + [vmem] * 6,
        out_specs=[vmem] * 2,
        out_shape=[shape((members, VARS, HALO, LANES), F32), tall],
        input_output_aliases={6: 1},
        scratch_shapes=[
            pltpu.VMEM((len(FORWARD), 24, LANES), F32),
            pltpu.VMEM((len(EVERY), ROWS, LANES), F32),
            pltpu.VMEM((TALL, LANES), F32),
        ],
        name="apply",
    )(class_rate, near(got), near(cls), near(below), near(above), near(own), near(spread))

    back = lax.all_to_all(part, "member", 0, 0, tiled=True)

    return pl.pallas_call(
        unpack_kernel,
        in_specs=[vmem],
        out_specs=vmem,
        out_shape=jax.ShapeDtypeStruct((1, VARS, LEV, ROWS, COLS), F32),
        name="unpack",
    )(near(back))


def solution(mesh):
    placed = (
        P("member", None, None, "row", "col"),
        P("member", None, None, "row", "col"),
        P("row", "col"),
        P(),
    )
    return jax.shard_map(
        body,
        mesh=mesh,
        in_specs=placed,
        out_specs=P("member", None, None, "row", "col"),
        check_vma=False,
    )
```

```python
import functools

import jax
import jax.numpy as jnp
from jax import lax
from jax.experimental import pallas as pl
from jax.experimental.pallas import tpu as pltpu
from jax.sharding import PartitionSpec as P

SWEEPS = 4
VARS = 3
LEV = 2
ROWS = 16
COLS = 512
HALO = 4
STRIP = 32
WIN = STRIP + 2 * HALO
LANES = 128
F32 = jnp.float32
BF16 = jnp.bfloat16


def grouped(a, b):
    upper = lax.broadcasted_iota(jnp.int32, (8, LANES), 0) < HALO
    groups = [
        jnp.where(upper, a[:8], pltpu.roll(b[:8], HALO, 0)),
        jnp.where(upper, pltpu.roll(a[8:], HALO, 0), b[8:]),
        jnp.where(upper, pltpu.roll(a[:8], HALO, 0), b[:8]),
        jnp.where(upper, a[8:], pltpu.roll(b[8:], HALO, 0)),
    ]
    return jnp.concatenate(groups, axis=0).astype(BF16)


def side_kernel(pert0_ref, pert1_ref, prob0_ref, prob1_ref, cls0_ref, cls1_ref, side_ref):
    last = lax.axis_index("col") == 0
    lane = lax.broadcasted_iota(jnp.int32, (ROWS, LANES), 1)
    use = [
        (lane >= WIN * v + jnp.where(last, 0, WIN - HALO)) & (lane < WIN * v + jnp.where(last, HALO, WIN))
        for v in range(VARS)
    ]

    def placed(blocks):
        acc = jnp.zeros((ROWS, LANES), F32)
        for v, (head, tail) in enumerate(blocks):
            tail = pltpu.roll(tail, (WIN * v + HALO) % LANES, 1)
            head = pltpu.roll(head, (WIN * v + WIN - HALO) % LANES, 1)
            acc = jnp.where(use[v], jnp.where(last, tail, head), acc)
        return acc

    for l in range(LEV):
        a, b = (
            placed([(head[0, v, l].astype(F32), tail[0, v, l].astype(F32)) for v in range(VARS)])
            for head, tail in ((pert0_ref, pert1_ref), (prob0_ref, prob1_ref))
        )
        side_ref[l * 2 * ROWS : (l + 1) * 2 * ROWS] = grouped(a, b)
    cls = ((cls0_ref[...] + 1).astype(F32), (cls1_ref[...] + 1).astype(F32))
    side_ref[LEV * 2 * ROWS :] = placed([cls] * VARS).astype(BF16)


def pack_kernel(pert_ref, prob_ref, cls_ref, out_ref, cls_out_ref, wide_ref):
    lane = lax.broadcasted_iota(jnp.int32, (ROWS, LANES), 1)
    blocks = COLS // LANES

    def block(ref, v, l, at, shift):
        got = ref[0, v, l, :, at * LANES : (at + 1) * LANES].astype(F32)
        return pltpu.roll(got, shift, 1) if shift else got

    for s in range(COLS // STRIP):
        start = s * STRIP - HALO
        at, off = start // LANES, start % LANES
        for l in range(LEV):
            both = []
            for ref in (pert_ref, prob_ref):
                acc = jnp.zeros((ROWS, LANES), F32)
                for v in range(VARS):
                    shift = (WIN * v - off) % LANES
                    low, high = WIN * v, WIN * (v + 1)
                    split = low + LANES - off
                    if at >= 0:
                        use = (lane >= low) & (lane < min(high, split))
                        acc = jnp.where(use, block(ref, v, l, at, shift), acc)
                    if split < high and at + 1 < blocks:
                        use = (lane >= split) & (lane < high)
                        acc = jnp.where(use, block(ref, v, l, at + 1, shift), acc)
                both.append(acc)
            out_ref[s * LEV + l] = grouped(*both)

    zero = jnp.zeros((ROWS, LANES), BF16)
    wide_ref[:, :LANES] = zero
    wide_ref[:, LANES : LANES + COLS] = (cls_ref[...] + 1).astype(F32).astype(BF16)
    wide_ref[:, LANES + COLS :] = zero
    strip = lax.axis_index("member") // LEV
    wide = wide_ref.shape[1]
    spot = lax.broadcasted_iota(jnp.int32, (wide, LANES), 0)
    lane = lax.broadcasted_iota(jnp.int32, (wide, LANES), 1)
    column = lane - jnp.where(lane >= WIN, WIN, 0) - jnp.where(lane >= 2 * WIN, WIN, 0)
    pick = (spot == LANES - HALO + STRIP * strip + column) & (lane < VARS * WIN)
    cls_out_ref[...] = jnp.dot(wide_ref[...], pick.astype(F32).astype(BF16), preferred_element_type=F32)


def patch_kernel(side_ref, inner_ref, cls_ref, out_ref, cls_out_ref):
    first = lax.axis_index("col") == 0
    strip = lax.axis_index("member") // LEV
    end = COLS // STRIP - 1
    for l in range(LEV):
        side = side_ref[l * 2 * ROWS : (l + 1) * 2 * ROWS].astype(F32)
        for s, here in ((0, jnp.logical_not(first)), (end, first)):
            at = s * LEV + l
            out_ref[at] = (inner_ref[at].astype(F32) + jnp.where(here, side, 0.0)).astype(BF16)
    mine = strip == jnp.where(first, end, 0)
    cls_out_ref[...] = cls_ref[...] + jnp.where(mine, side_ref[LEV * 2 * ROWS :].astype(F32), 0.0)


def edge_kernel(got_ref, cls_ref, up_ref, dn_ref):
    members = got_ref.shape[0]
    up_ref[:members] = got_ref[:, :8]
    dn_ref[:members] = got_ref[:, 8:16]
    up_ref[members] = cls_ref[:8].astype(BF16)
    dn_ref[members] = pltpu.roll(cls_ref[8:], HALO, 0).astype(BF16)


TOP = 8
TALL = TOP + ROWS + TOP
FORWARD = [
    (dy, dx)
    for dy in range(HALO + 1)
    for dx in range(-HALO, HALO + 1)
    if dy + abs(dx) <= HALO and (dy > 0 or dx >= 0)
]
EVERY = [(dy, dx) for dx in range(-HALO, HALO + 1) for dy in range(-HALO, HALO + 1) if abs(dy) + abs(dx) <= HALO]
AT = {d: i for i, d in enumerate(EVERY)}


def lanes_by(x, dx):
    return pltpu.roll(x, (-dx) % LANES, 1) if dx else x


def own_kernel(got_ref, gram_ref, prob_ref, pert_ref):
    members = got_ref.shape[0]
    blank = jnp.zeros((TOP, LANES), F32)

    def spread(m, _):
        tile = got_ref[m].astype(F32)
        pert_ref[m, 0:TOP] = blank
        for group, to in enumerate((0, 12, 4, 8)):
            pert_ref[m, TOP + to : TOP + to + HALO] = tile[8 * group : 8 * group + HALO]
            prob_ref[m, TOP + to : TOP + to + HALO] = tile[8 * group + HALO : 8 * group + 8]
        return 0

    lax.fori_loop(0, members, spread, 0, unroll=4)
    for b in range(2):
        row = TOP + 8 * b

        def products(m, acc):
            low = pert_ref[m, row : row + 8]
            high = [pert_ref[m, row - dy : row - dy + 8] for dy in range(HALO + 1)]
            near = {dx: lanes_by(low, dx) for dx in range(-HALO + 1, HALO + 1)}
            return tuple(a + high[dy] * near[dx] for a, (dy, dx) in zip(acc, FORWARD))

        acc = tuple(jnp.zeros((8, LANES), F32) for _ in FORWARD)
        acc = lax.fori_loop(0, members, products, acc, unroll=4)
        for i, a in enumerate(acc):
            gram_ref[i, 8 * b : 8 * b + 8] = a


def apply_kernel(
    n_row, rates_ref, got_ref, cls_ref, below_ref, above_ref, own_ref, part_ref, out_ref,
    prob_ref, gram_ref, weight_ref, rate_ref,
):
    members = got_ref.shape[0]
    has_below = lax.axis_index("row") != n_row - 1
    has_above = lax.axis_index("row") != 0
    blank = jnp.zeros((HALO, LANES), F32)
    sub = lax.broadcasted_iota(jnp.int32, (8, LANES), 0)
    lane = lax.broadcasted_iota(jnp.int32, (8, LANES), 1)
    upper = sub < HALO
    crossing = [d for d in FORWARD if d[0] > 0]

    def spread(m, acc):
        tile = got_ref[m, :ROWS].astype(F32)
        below, above = below_ref[m].astype(F32), above_ref[m].astype(F32)
        prob_ref[m, TOP - HALO : TOP] = above[HALO:]
        prob_ref[m, TOP + ROWS : TOP + ROWS + HALO] = below[HALO:]
        low = jnp.where(upper, tile[0:8], pltpu.roll(below, HALO, 0))
        high = jnp.where(upper, above, pltpu.roll(tile[8:16], HALO, 0))
        high = {dy: pltpu.roll(high, HALO + dy, 0) if dy < HALO else high for dy in range(1, HALO + 1)}
        near = {dx: lanes_by(low, dx) for dx in range(-HALO + 1, HALO)}
        return tuple(a + high[dy] * near[dx] for a, (dy, dx) in zip(acc, crossing))

    acc = tuple(jnp.zeros((8, LANES), F32) for _ in crossing)
    acc = lax.fori_loop(0, members, spread, acc, unroll=4)
    inside = (upper & has_above) | (jnp.logical_not(upper) & has_below)
    acc = {d: jnp.where(inside, a, 0.0) for d, a in zip(crossing, acc)}
    for i, d in enumerate(FORWARD):
        gram_ref[i, 8:16] = own_ref[i, 8:16]
        if d in acc:
            gram_ref[i, 0:8] = own_ref[i, 0:8] + jnp.where(sub < d[0], acc[d], 0.0)
            gram_ref[i, 16:24] = pltpu.roll(acc[d], HALO, 0)
        else:
            gram_ref[i, 0:8] = own_ref[i, 0:8]

    cls = jnp.concatenate(
        [
            blank,
            jnp.where(has_above, above_ref[members, :HALO].astype(F32), 0.0),
            cls_ref[...],
            jnp.where(has_below, below_ref[members, :HALO].astype(F32), 0.0),
            blank,
        ],
        axis=0,
    )
    rate = jnp.zeros((TALL, LANES), F32)
    for k in range(rates_ref.shape[0]):
        rate = jnp.where(cls == float(k + 1), rates_ref[k], rate)
    rate_ref[...] = rate

    steps = ((0, 1), (0, -1), (1, 0), (-1, 0))
    scale = 1.0 / (members - 1)
    for b in range(2):
        at = {
            (dy, dx): lanes_by(rate_ref[TOP + 8 * b + dy : TOP + 8 * b + dy + 8], dx)
            for dy, dx in EVERY
            if abs(dy) + abs(dx) < HALO
        }
        coef = {(0, 0): 1.0 - 4.0 * at[(0, 0)]}
        for e in steps:
            coef[e] = at[(0, 0)]
        for sweep in range(1, SWEEPS):
            flow = {d: c * at[d] for d, c in coef.items()}
            to = {(d[0] + e[0], d[1] + e[1]) for d in flow for e in steps}
            new = {}
            for d in EVERY:
                if d not in to:
                    continue
                terms = [flow[(d[0] - e[0], d[1] - e[1])] for e in steps if (d[0] - e[0], d[1] - e[1]) in flow]
                if d in coef:
                    terms.append(coef[d] - 4.0 * flow[d])
                total = terms[0]
                for t in terms[1:]:
                    total = total + t
                new[d] = total
            coef = new
        rows = slice(8 * b, 8 * b + 8)
        for i, (dy, dx) in enumerate(FORWARD):
            gram = gram_ref[i, 8 * b + dy : 8 * b + dy + 8]
            weight_ref[AT[(dy, dx)], rows] = lanes_by(coef[(dy, dx)] * scale * gram, -dx)
            if (dy, dx) != (0, 0):
                weight_ref[AT[(-dy, -dx)], rows] = lanes_by(coef[(-dy, -dx)] * scale, dx) * gram_ref[i, rows]

    def sums(pair):
        both = [[], []]
        for b in range(2):
            rows = [
                [prob_ref[p, TOP + 8 * b + dy : TOP + 8 * b + dy + 8] for dy in range(-HALO, HALO + 1)] for p in pair
            ]
            total = [None, None]
            for dx in range(-HALO, HALO + 1):
                part = [None, None]
                for dy in range(-HALO + abs(dx), HALO - abs(dx) + 1):
                    weight = weight_ref[AT[(dy, dx)], 8 * b : 8 * b + 8]
                    for j in range(2):
                        term = weight * rows[j][dy + HALO]
                        part[j] = term if part[j] is None else part[j] + term
                for j in range(2):
                    moved = lanes_by(part[j], dx)
                    total[j] = moved if total[j] is None else total[j] + moved
            for j in range(2):
                both[j].append(total[j])
        return tuple(both[0] + both[1])

    def store(pair, done):
        for p, a, b in ((pair[0], done[0], done[1]), (pair[1], done[2], done[3])):
            first = jnp.where(lane < STRIP, lanes_by(a, HALO), lanes_by(a, HALO + 8))
            first = jnp.where(lane < 2 * STRIP, first, lanes_by(a, HALO + 16))
            first = jnp.where(lane < 3 * STRIP, first, lanes_by(b, HALO - 3 * STRIP))
            rest = jnp.where(lane < STRIP, lanes_by(b, WIN + HALO), lanes_by(b, 2 * WIN + HALO - STRIP))
            rest = jnp.where(lane < 2 * STRIP, rest, pltpu.roll(lanes_by(rest, 2 * STRIP), HALO, 0))
            out_ref[p, 0] = first[:HALO]
            out_ref[p, 1] = first[HALO:]
            out_ref[p, 2] = rest[:HALO]

    def step(i, _):
        pair = (2 * i, 2 * i + 1)
        store(pair, sums(pair))
        return 0

    lax.fori_loop(0, members // 2, step, 0, unroll=4)


def unpack_kernel(got_ref, out_ref):
    lane = lax.broadcasted_iota(jnp.int32, (ROWS, LANES), 1)
    per = LANES // STRIP

    def moved(x, shift):
        shift %= LANES
        return pltpu.roll(x, shift, 1) if shift else x

    for l in range(LEV):
        for at in range(COLS // LANES):
            acc = [None] * VARS
            for q in range(per):
                got = got_ref[(at * per + q) * LEV + l]
                top = jnp.concatenate([got[0], got[1]], axis=0)
                low = jnp.concatenate([got[2], moved(got[2], 2 * STRIP)], axis=0)
                for v in range(VARS):
                    under = moved(top, STRIP * (q - VARS)) if v == 0 else moved(low, STRIP * (q - v + 1))
                    piece = jnp.concatenate([moved(top, STRIP * (q - v)), under], axis=0)
                    acc[v] = piece if acc[v] is None else jnp.where(lane >= STRIP * q, piece, acc[v])
            for v in range(VARS):
                out_ref[0, v, l, :, at * LANES : (at + 1) * LANES] = acc[v]


def body(pert, probes, diff_class, class_rate):
    members = lax.axis_size("member")
    n_row = lax.axis_size("row")
    vmem = pl.BlockSpec(memory_space=pltpu.VMEM)
    smem = pl.BlockSpec(memory_space=pltpu.SMEM)
    shape = pltpu.VMEM

    def near(x):
        return pltpu.with_memory_space_constraint(x, pltpu.VMEM)

    ends = (0, COLS // LANES - 1)
    tile = [pl.BlockSpec((1, VARS, LEV, ROWS, LANES), functools.partial(lambda at, i: (0, 0, 0, 0, at), at)) for at in ends]
    plane = [pl.BlockSpec((ROWS, LANES), functools.partial(lambda at, i: (0, at), at)) for at in ends]
    side = pl.pallas_call(
        side_kernel,
        grid=(1,),
        in_specs=tile + tile + plane,
        out_specs=vmem,
        out_shape=shape(((2 * LEV + 1) * ROWS, LANES), BF16),
        name="side",
    )(pert, pert, probes, probes, diff_class, diff_class)
    beside = lax.ppermute(side, "col", [(0, 1), (1, 0)])

    chunk, classes = shape((members, 2 * ROWS, LANES), BF16), shape((ROWS, LANES), F32)
    inner, cls = pl.pallas_call(
        pack_kernel,
        in_specs=[vmem] * 3,
        out_specs=[vmem] * 2,
        out_shape=[chunk, classes],
        scratch_shapes=[pltpu.VMEM((ROWS, COLS + 2 * LANES), BF16)],
        name="pack",
    )(pert, probes, diff_class)
    chunks, cls = pl.pallas_call(
        patch_kernel,
        in_specs=[vmem] * 3,
        out_specs=[vmem] * 2,
        out_shape=[chunk, classes],
        input_output_aliases={1: 0},
        name="patch",
    )(near(beside), near(inner), near(cls))

    got = lax.all_to_all(chunks, "member", 0, 0, tiled=True)

    edge = shape((members + 1, 8, LANES), BF16)
    up, dn = pl.pallas_call(
        edge_kernel,
        in_specs=[vmem] * 2,
        out_specs=[vmem] * 2,
        out_shape=[edge, edge],
        name="edges",
    )(near(got), near(cls))
    below = lax.ppermute(up, "row", [(i, (i - 1) % n_row) for i in range(n_row)])
    above = lax.ppermute(dn, "row", [(i, (i + 1) % n_row) for i in range(n_row)])

    tall = shape((members, TALL, LANES), F32)
    own, spread = pl.pallas_call(
        own_kernel,
        in_specs=[vmem],
        out_specs=[vmem] * 2,
        out_shape=[shape((len(FORWARD), ROWS, LANES), F32), tall],
        scratch_shapes=[pltpu.VMEM((members, TOP + ROWS, LANES), F32)],
        name="own",
    )(near(got))

    part, spread = pl.pallas_call(
        functools.partial(apply_kernel, n_row),
        in_specs=[smem] + [vmem] * 6,
        out_specs=[vmem] * 2,
        out_shape=[shape((members, VARS, HALO, LANES), F32), tall],
        input_output_aliases={6: 1},
        scratch_shapes=[
            pltpu.VMEM((len(FORWARD), 24, LANES), F32),
            pltpu.VMEM((len(EVERY), ROWS, LANES), F32),
            pltpu.VMEM((TALL, LANES), F32),
        ],
        name="apply",
    )(class_rate, near(got), near(cls), near(below), near(above), near(own), near(spread))

    back = lax.all_to_all(part, "member", 0, 0, tiled=True)

    return pl.pallas_call(
        unpack_kernel,
        in_specs=[vmem],
        out_specs=vmem,
        out_shape=jax.ShapeDtypeStruct((1, VARS, LEV, ROWS, COLS), F32),
        name="unpack",
    )(near(back))


def solution(mesh):
    placed = (
        P("member", None, None, "row", "col"),
        P("member", None, None, "row", "col"),
        P("row", "col"),
        P(),
    )
    return jax.shard_map(
        body,
        mesh=mesh,
        in_specs=placed,
        out_specs=P("member", None, None, "row", "col"),
        check_vma=False,
    )
```

```python
import functools

import jax
import jax.numpy as jnp
from jax import lax
from jax.experimental import pallas as pl
from jax.experimental.pallas import tpu as pltpu
from jax.sharding import PartitionSpec as P

SWEEPS = 4
VARS = 3
LEV = 2
ROWS = 16
COLS = 512
HALO = 4
STRIP = 32
WIN = STRIP + 2 * HALO
LANES = 128
F32 = jnp.float32
BF16 = jnp.bfloat16


def grouped(a, b):
    upper = lax.broadcasted_iota(jnp.int32, (8, LANES), 0) < HALO
    groups = [
        jnp.where(upper, a[:8], pltpu.roll(b[:8], HALO, 0)),
        jnp.where(upper, pltpu.roll(a[8:], HALO, 0), b[8:]),
        jnp.where(upper, pltpu.roll(a[:8], HALO, 0), b[:8]),
        jnp.where(upper, a[8:], pltpu.roll(b[8:], HALO, 0)),
    ]
    return jnp.concatenate(groups, axis=0).astype(BF16)


def side_kernel(pert0_ref, pert1_ref, prob0_ref, prob1_ref, cls0_ref, cls1_ref, side_ref):
    last = lax.axis_index("col") == 0
    lane = lax.broadcasted_iota(jnp.int32, (ROWS, LANES), 1)
    use = [
        (lane >= WIN * v + jnp.where(last, 0, WIN - HALO)) & (lane < WIN * v + jnp.where(last, HALO, WIN))
        for v in range(VARS)
    ]

    def placed(blocks):
        acc = jnp.zeros((ROWS, LANES), F32)
        for v, (head, tail) in enumerate(blocks):
            tail = pltpu.roll(tail, (WIN * v + HALO) % LANES, 1)
            head = pltpu.roll(head, (WIN * v + WIN - HALO) % LANES, 1)
            acc = jnp.where(use[v], jnp.where(last, tail, head), acc)
        return acc

    for l in range(LEV):
        a, b = (
            placed([(head[0, v, l].astype(F32), tail[0, v, l].astype(F32)) for v in range(VARS)])
            for head, tail in ((pert0_ref, pert1_ref), (prob0_ref, prob1_ref))
        )
        side_ref[l * 2 * ROWS : (l + 1) * 2 * ROWS] = grouped(a, b)
    cls = ((cls0_ref[...] + 1).astype(F32), (cls1_ref[...] + 1).astype(F32))
    side_ref[LEV * 2 * ROWS :] = placed([cls] * VARS).astype(BF16)


def pack_kernel(pert_ref, prob_ref, cls_ref, out_ref, cls_out_ref, wide_ref):
    lane = lax.broadcasted_iota(jnp.int32, (ROWS, LANES), 1)
    blocks = COLS // LANES

    def block(ref, v, l, at, shift):
        got = ref[0, v, l, :, at * LANES : (at + 1) * LANES].astype(F32)
        return pltpu.roll(got, shift, 1) if shift else got

    for s in range(COLS // STRIP):
        start = s * STRIP - HALO
        at, off = start // LANES, start % LANES
        for l in range(LEV):
            both = []
            for ref in (pert_ref, prob_ref):
                acc = jnp.zeros((ROWS, LANES), F32)
                for v in range(VARS):
                    shift = (WIN * v - off) % LANES
                    low, high = WIN * v, WIN * (v + 1)
                    split = low + LANES - off
                    if at >= 0:
                        use = (lane >= low) & (lane < min(high, split))
                        acc = jnp.where(use, block(ref, v, l, at, shift), acc)
                    if split < high and at + 1 < blocks:
                        use = (lane >= split) & (lane < high)
                        acc = jnp.where(use, block(ref, v, l, at + 1, shift), acc)
                both.append(acc)
            out_ref[s * LEV + l] = grouped(*both)

    zero = jnp.zeros((ROWS, LANES), BF16)
    wide_ref[:, :LANES] = zero
    wide_ref[:, LANES : LANES + COLS] = (cls_ref[...] + 1).astype(F32).astype(BF16)
    wide_ref[:, LANES + COLS :] = zero
    strip = lax.axis_index("member") // LEV
    wide = wide_ref.shape[1]
    spot = lax.broadcasted_iota(jnp.int32, (wide, LANES), 0)
    lane = lax.broadcasted_iota(jnp.int32, (wide, LANES), 1)
    column = lane - jnp.where(lane >= WIN, WIN, 0) - jnp.where(lane >= 2 * WIN, WIN, 0)
    pick = (spot == LANES - HALO + STRIP * strip + column) & (lane < VARS * WIN)
    cls_out_ref[...] = jnp.dot(wide_ref[...], pick.astype(F32).astype(BF16), preferred_element_type=F32)


def patch_kernel(side_ref, inner_ref, cls_ref, out_ref, cls_out_ref):
    first = lax.axis_index("col") == 0
    strip = lax.axis_index("member") // LEV
    end = COLS // STRIP - 1
    for l in range(LEV):
        side = side_ref[l * 2 * ROWS : (l + 1) * 2 * ROWS].astype(F32)
        for s, here in ((0, jnp.logical_not(first)), (end, first)):
            at = s * LEV + l
            out_ref[at] = (inner_ref[at].astype(F32) + jnp.where(here, side, 0.0)).astype(BF16)
    mine = strip == jnp.where(first, end, 0)
    cls_out_ref[...] = cls_ref[...] + jnp.where(mine, side_ref[LEV * 2 * ROWS :].astype(F32), 0.0)


def edge_kernel(got_ref, cls_ref, up_ref, dn_ref):
    members = got_ref.shape[0]
    up_ref[:members] = got_ref[:, :8]
    dn_ref[:members] = got_ref[:, 8:16]
    up_ref[members] = cls_ref[:8].astype(BF16)
    dn_ref[members] = pltpu.roll(cls_ref[8:], HALO, 0).astype(BF16)


TOP = 8
TALL = TOP + ROWS + TOP
FORWARD = [
    (dy, dx)
    for dy in range(HALO + 1)
    for dx in range(-HALO, HALO + 1)
    if dy + abs(dx) <= HALO and (dy > 0 or dx >= 0)
]
EVERY = [(dy, dx) for dx in range(-HALO, HALO + 1) for dy in range(-HALO, HALO + 1) if abs(dy) + abs(dx) <= HALO]
AT = {d: i for i, d in enumerate(EVERY)}


def lanes_by(x, dx):
    return pltpu.roll(x, (-dx) % LANES, 1) if dx else x


def own_kernel(got_ref, gram_ref, prob_ref, pert_ref):
    members = got_ref.shape[0]
    blank = jnp.zeros((TOP, LANES), F32)

    def spread(m, _):
        tile = got_ref[m].astype(F32)
        pert_ref[m, 0:TOP] = blank
        for group, to in enumerate((0, 12, 4, 8)):
            pert_ref[m, TOP + to : TOP + to + HALO] = tile[8 * group : 8 * group + HALO]
            prob_ref[m, TOP + to : TOP + to + HALO] = tile[8 * group + HALO : 8 * group + 8]
        return 0

    lax.fori_loop(0, members, spread, 0, unroll=4)
    for b in range(2):
        row = TOP + 8 * b

        def products(m, acc):
            low = pert_ref[m, row : row + 8]
            high = [pert_ref[m, row - dy : row - dy + 8] for dy in range(HALO + 1)]
            near = {dx: lanes_by(low, dx) for dx in range(-HALO + 1, HALO + 1)}
            return tuple(a + high[dy] * near[dx] for a, (dy, dx) in zip(acc, FORWARD))

        acc = tuple(jnp.zeros((8, LANES), F32) for _ in FORWARD)
        acc = lax.fori_loop(0, members, products, acc, unroll=4)
        for i, a in enumerate(acc):
            gram_ref[i, 8 * b : 8 * b + 8] = a


def apply_kernel(
    n_row, rates_ref, got_ref, cls_ref, below_ref, above_ref, own_ref, part_ref, out_ref,
    prob_ref, gram_ref, weight_ref, rate_ref,
):
    members = got_ref.shape[0]
    has_below = lax.axis_index("row") != n_row - 1
    has_above = lax.axis_index("row") != 0
    blank = jnp.zeros((HALO, LANES), F32)
    sub = lax.broadcasted_iota(jnp.int32, (8, LANES), 0)
    lane = lax.broadcasted_iota(jnp.int32, (8, LANES), 1)
    upper = sub < HALO
    crossing = [d for d in FORWARD if d[0] > 0]

    def spread(m, acc):
        tile = got_ref[m, :ROWS].astype(F32)
        below, above = below_ref[m].astype(F32), above_ref[m].astype(F32)
        prob_ref[m, TOP - HALO : TOP] = above[HALO:]
        prob_ref[m, TOP + ROWS : TOP + ROWS + HALO] = below[HALO:]
        low = jnp.where(upper, tile[0:8], pltpu.roll(below, HALO, 0))
        high = jnp.where(upper, above, pltpu.roll(tile[8:16], HALO, 0))
        high = {dy: pltpu.roll(high, HALO + dy, 0) if dy < HALO else high for dy in range(1, HALO + 1)}
        near = {dx: lanes_by(low, dx) for dx in range(-HALO + 1, HALO)}
        return tuple(a + high[dy] * near[dx] for a, (dy, dx) in zip(acc, crossing))

    acc = tuple(jnp.zeros((8, LANES), F32) for _ in crossing)
    acc = lax.fori_loop(0, members, spread, acc, unroll=4)
    inside = (upper & has_above) | (jnp.logical_not(upper) & has_below)
    acc = {d: jnp.where(inside, a, 0.0) for d, a in zip(crossing, acc)}
    for i, d in enumerate(FORWARD):
        gram_ref[i, 8:16] = own_ref[i, 8:16]
        if d in acc:
            gram_ref[i, 0:8] = own_ref[i, 0:8] + jnp.where(sub < d[0], acc[d], 0.0)
            gram_ref[i, 16:24] = pltpu.roll(acc[d], HALO, 0)
        else:
            gram_ref[i, 0:8] = own_ref[i, 0:8]

    cls = jnp.concatenate(
        [
            blank,
            jnp.where(has_above, above_ref[members, :HALO].astype(F32), 0.0),
            cls_ref[...],
            jnp.where(has_below, below_ref[members, :HALO].astype(F32), 0.0),
            blank,
        ],
        axis=0,
    )
    rate = jnp.zeros((TALL, LANES), F32)
    for k in range(rates_ref.shape[0]):
        rate = jnp.where(cls == float(k + 1), rates_ref[k], rate)
    rate_ref[...] = rate

    steps = ((0, 1), (0, -1), (1, 0), (-1, 0))
    scale = 1.0 / (members - 1)
    for b in range(2):
        at = {
            (dy, dx): lanes_by(rate_ref[TOP + 8 * b + dy : TOP + 8 * b + dy + 8], dx)
            for dy, dx in EVERY
            if abs(dy) + abs(dx) < HALO
        }
        coef = {(0, 0): 1.0 - 4.0 * at[(0, 0)]}
        for e in steps:
            coef[e] = at[(0, 0)]
        for sweep in range(1, SWEEPS):
            flow = {d: c * at[d] for d, c in coef.items()}
            to = {(d[0] + e[0], d[1] + e[1]) for d in flow for e in steps}
            new = {}
            for d in EVERY:
                if d not in to:
                    continue
                terms = [flow[(d[0] - e[0], d[1] - e[1])] for e in steps if (d[0] - e[0], d[1] - e[1]) in flow]
                if d in coef:
                    terms.append(coef[d] - 4.0 * flow[d])
                total = terms[0]
                for t in terms[1:]:
                    total = total + t
                new[d] = total
            coef = new
        rows = slice(8 * b, 8 * b + 8)
        for i, (dy, dx) in enumerate(FORWARD):
            gram = gram_ref[i, 8 * b + dy : 8 * b + dy + 8]
            weight_ref[AT[(dy, dx)], rows] = lanes_by(coef[(dy, dx)] * scale * gram, -dx)
            if (dy, dx) != (0, 0):
                weight_ref[AT[(-dy, -dx)], rows] = lanes_by(coef[(-dy, -dx)] * scale, dx) * gram_ref[i, rows]

    def sums(pair):
        both = [[], []]
        for b in range(2):
            rows = [
                [prob_ref[p, TOP + 8 * b + dy : TOP + 8 * b + dy + 8] for dy in range(-HALO, HALO + 1)] for p in pair
            ]
            total = [None, None]
            for dx in range(-HALO, HALO + 1):
                part = [None, None]
                for dy in range(-HALO + abs(dx), HALO - abs(dx) + 1):
                    weight = weight_ref[AT[(dy, dx)], 8 * b : 8 * b + 8]
                    for j in range(2):
                        term = weight * rows[j][dy + HALO]
                        part[j] = term if part[j] is None else part[j] + term
                for j in range(2):
                    moved = lanes_by(part[j], dx)
                    total[j] = moved if total[j] is None else total[j] + moved
            for j in range(2):
                both[j].append(total[j])
        return tuple(both[0] + both[1])

    turn = lax.axis_index("member") // LEV % (LANES // STRIP) * STRIP
    slot = (lane - turn) & (LANES - 1)

    def turned(x, dx):
        return pltpu.roll(x, (turn + (-dx) % LANES) & (LANES - 1), 1)

    def store(pair, done):
        for p, a, b in ((pair[0], done[0], done[1]), (pair[1], done[2], done[3])):
            first = jnp.where(slot < STRIP, turned(a, HALO), turned(a, HALO + 8))
            first = jnp.where(slot < 2 * STRIP, first, turned(a, HALO + 16))
            first = jnp.where(slot < 3 * STRIP, first, turned(b, HALO - 3 * STRIP))
            rest = jnp.where(slot < STRIP, turned(b, WIN + HALO), turned(b, 2 * WIN + HALO - STRIP))
            rest = jnp.where(slot < 2 * STRIP, rest, pltpu.roll(lanes_by(rest, 2 * STRIP), HALO, 0))
            out_ref[p, 0] = first[:HALO]
            out_ref[p, 1] = first[HALO:]
            out_ref[p, 2] = rest[:HALO]

    def step(i, _):
        pair = (2 * i, 2 * i + 1)
        store(pair, sums(pair))
        return 0

    lax.fori_loop(0, members // 2, step, 0, unroll=4)


def unpack_kernel(got_ref, out_ref, tile_ref, sems):
    per = LANES // STRIP
    blocks = COLS // LANES
    slots = [lax.broadcasted_iota(jnp.int32, (rows, LANES), 1) // STRIP for rows in (HALO, 8)]

    def joined(parts, first):
        slot = slots[0] if parts[0].shape[0] == HALO else slots[1]
        acc = parts[0]
        for q in range(1, per):
            acc = jnp.where(slot == (first + q) % per, parts[q], acc)
        return pltpu.roll(acc, (-first * STRIP) % LANES, 1) if first % per else acc

    copies = []
    for l in range(LEV):
        for at in range(blocks):
            got = [got_ref[(at * per + q) * LEV + l] for q in range(per)]
            top = [jnp.concatenate([g[0], g[1]], axis=0) for g in got]
            low = [g[2] for g in got]
            span = slice(at * LANES, (at + 1) * LANES)
            for v in range(VARS):
                tile_ref[v, l, :8, span] = joined(top, v)
                if v == 0:
                    tile_ref[v, l, 8:, span] = joined(top, VARS)
                else:
                    tile_ref[v, l, 8 : 8 + HALO, span] = joined(low, v - 1)
                    tile_ref[v, l, 8 + HALO :, span] = joined(low, v + 1)
        for v in range(VARS):
            copy = pltpu.make_async_copy(tile_ref.at[v, l], out_ref.at[0, v, l], sems.at[v * LEV + l])
            copy.start()
            copies.append(copy)
    for copy in copies:
        copy.wait()


def body(pert, probes, diff_class, class_rate):
    members = lax.axis_size("member")
    n_row = lax.axis_size("row")
    vmem = pl.BlockSpec(memory_space=pltpu.VMEM)
    smem = pl.BlockSpec(memory_space=pltpu.SMEM)
    shape = pltpu.VMEM

    def near(x):
        return pltpu.with_memory_space_constraint(x, pltpu.VMEM)

    ends = (0, COLS // LANES - 1)
    tile = [pl.BlockSpec((1, VARS, LEV, ROWS, LANES), functools.partial(lambda at, i: (0, 0, 0, 0, at), at)) for at in ends]
    plane = [pl.BlockSpec((ROWS, LANES), functools.partial(lambda at, i: (0, at), at)) for at in ends]
    side = pl.pallas_call(
        side_kernel,
        grid=(1,),
        in_specs=tile + tile + plane,
        out_specs=vmem,
        out_shape=shape(((2 * LEV + 1) * ROWS, LANES), BF16),
        name="side",
    )(pert, pert, probes, probes, diff_class, diff_class)
    beside = lax.ppermute(side, "col", [(0, 1), (1, 0)])

    chunk, classes = shape((members, 2 * ROWS, LANES), BF16), shape((ROWS, LANES), F32)
    inner, cls = pl.pallas_call(
        pack_kernel,
        in_specs=[vmem] * 3,
        out_specs=[vmem] * 2,
        out_shape=[chunk, classes],
        scratch_shapes=[pltpu.VMEM((ROWS, COLS + 2 * LANES), BF16)],
        name="pack",
    )(pert, probes, diff_class)
    chunks, cls = pl.pallas_call(
        patch_kernel,
        in_specs=[vmem] * 3,
        out_specs=[vmem] * 2,
        out_shape=[chunk, classes],
        input_output_aliases={1: 0},
        name="patch",
    )(near(beside), near(inner), near(cls))

    got = lax.all_to_all(chunks, "member", 0, 0, tiled=True)

    edge = shape((members + 1, 8, LANES), BF16)
    up, dn = pl.pallas_call(
        edge_kernel,
        in_specs=[vmem] * 2,
        out_specs=[vmem] * 2,
        out_shape=[edge, edge],
        name="edges",
    )(near(got), near(cls))
    below = lax.ppermute(up, "row", [(i, (i - 1) % n_row) for i in range(n_row)])
    above = lax.ppermute(dn, "row", [(i, (i + 1) % n_row) for i in range(n_row)])

    tall = shape((members, TALL, LANES), F32)
    own, spread = pl.pallas_call(
        own_kernel,
        in_specs=[vmem],
        out_specs=[vmem] * 2,
        out_shape=[shape((len(FORWARD), ROWS, LANES), F32), tall],
        scratch_shapes=[pltpu.VMEM((members, TOP + ROWS, LANES), F32)],
        name="own",
    )(near(got))

    part, spread = pl.pallas_call(
        functools.partial(apply_kernel, n_row),
        in_specs=[smem] + [vmem] * 6,
        out_specs=[vmem] * 2,
        out_shape=[shape((members, VARS, HALO, LANES), F32), tall],
        input_output_aliases={6: 1},
        scratch_shapes=[
            pltpu.VMEM((len(FORWARD), 24, LANES), F32),
            pltpu.VMEM((len(EVERY), ROWS, LANES), F32),
            pltpu.VMEM((TALL, LANES), F32),
        ],
        name="apply",
    )(class_rate, near(got), near(cls), near(below), near(above), near(own), near(spread))

    back = lax.all_to_all(part, "member", 0, 0, tiled=True)

    return pl.pallas_call(
        unpack_kernel,
        in_specs=[vmem],
        out_specs=pl.BlockSpec(memory_space=pl.ANY),
        out_shape=jax.ShapeDtypeStruct((1, VARS, LEV, ROWS, COLS), F32),
        scratch_shapes=[
            pltpu.VMEM((VARS, LEV, ROWS, COLS), F32),
            pltpu.SemaphoreType.DMA((VARS * LEV,)),
        ],
        name="unpack",
    )(near(back))


def solution(mesh):
    placed = (
        P("member", None, None, "row", "col"),
        P("member", None, None, "row", "col"),
        P("row", "col"),
        P(),
    )
    return jax.shard_map(
        body,
        mesh=mesh,
        in_specs=placed,
        out_specs=P("member", None, None, "row", "col"),
        check_vma=False,
    )
```

```python
import functools

import jax
import jax.numpy as jnp
from jax import lax
from jax.experimental import pallas as pl
from jax.experimental.pallas import tpu as pltpu
from jax.sharding import PartitionSpec as P

SWEEPS = 4
VARS = 3
LEV = 2
ROWS = 16
COLS = 512
HALO = 4
STRIP = 32
WIN = STRIP + 2 * HALO
LANES = 128
F32 = jnp.float32
BF16 = jnp.bfloat16


def grouped(a, b):
    upper = lax.broadcasted_iota(jnp.int32, (8, LANES), 0) < HALO
    groups = [
        jnp.where(upper, a[:8], pltpu.roll(b[:8], HALO, 0)),
        jnp.where(upper, pltpu.roll(a[8:], HALO, 0), b[8:]),
        jnp.where(upper, pltpu.roll(a[:8], HALO, 0), b[:8]),
        jnp.where(upper, a[8:], pltpu.roll(b[8:], HALO, 0)),
    ]
    return jnp.concatenate(groups, axis=0).astype(BF16)


def side_kernel(pert0_ref, pert1_ref, prob0_ref, prob1_ref, cls0_ref, cls1_ref, side_ref):
    last = lax.axis_index("col") == 0
    lane = lax.broadcasted_iota(jnp.int32, (ROWS, LANES), 1)
    use = [
        (lane >= WIN * v + jnp.where(last, 0, WIN - HALO)) & (lane < WIN * v + jnp.where(last, HALO, WIN))
        for v in range(VARS)
    ]

    def placed(blocks):
        acc = jnp.zeros((ROWS, LANES), F32)
        for v, (head, tail) in enumerate(blocks):
            tail = pltpu.roll(tail, (WIN * v + HALO) % LANES, 1)
            head = pltpu.roll(head, (WIN * v + WIN - HALO) % LANES, 1)
            acc = jnp.where(use[v], jnp.where(last, tail, head), acc)
        return acc

    for l in range(LEV):
        a, b = (
            placed([(head[0, v, l].astype(F32), tail[0, v, l].astype(F32)) for v in range(VARS)])
            for head, tail in ((pert0_ref, pert1_ref), (prob0_ref, prob1_ref))
        )
        side_ref[l * 2 * ROWS : (l + 1) * 2 * ROWS] = grouped(a, b)
    cls = ((cls0_ref[...] + 1).astype(F32), (cls1_ref[...] + 1).astype(F32))
    side_ref[LEV * 2 * ROWS :] = placed([cls] * VARS).astype(BF16)


def pack_kernel(rates_ref, pert_ref, prob_ref, cls_ref, out_ref, cls_out_ref, rates_out_ref, wide_ref):
    lane = lax.broadcasted_iota(jnp.int32, (ROWS, LANES), 1)
    blocks = COLS // LANES
    for k in range(rates_ref.shape[0]):
        rates_out_ref[k : k + 1] = jnp.full((1, LANES), rates_ref[k], F32)

    def block(ref, v, l, at, shift):
        got = ref[0, v, l, :, at * LANES : (at + 1) * LANES].astype(F32)
        return pltpu.roll(got, shift, 1) if shift else got

    for s in range(COLS // STRIP):
        start = s * STRIP - HALO
        at, off = start // LANES, start % LANES
        for l in range(LEV):
            both = []
            for ref in (pert_ref, prob_ref):
                acc = jnp.zeros((ROWS, LANES), F32)
                for v in range(VARS):
                    shift = (WIN * v - off) % LANES
                    low, high = WIN * v, WIN * (v + 1)
                    split = low + LANES - off
                    if at >= 0:
                        use = (lane >= low) & (lane < min(high, split))
                        acc = jnp.where(use, block(ref, v, l, at, shift), acc)
                    if split < high and at + 1 < blocks:
                        use = (lane >= split) & (lane < high)
                        acc = jnp.where(use, block(ref, v, l, at + 1, shift), acc)
                both.append(acc)
            out_ref[s * LEV + l] = grouped(*both)

    zero = jnp.zeros((ROWS, LANES), BF16)
    wide_ref[:, :LANES] = zero
    wide_ref[:, LANES : LANES + COLS] = (cls_ref[...] + 1).astype(F32).astype(BF16)
    wide_ref[:, LANES + COLS :] = zero
    strip = lax.axis_index("member") // LEV
    wide = wide_ref.shape[1]
    spot = lax.broadcasted_iota(jnp.int32, (wide, LANES), 0)
    lane = lax.broadcasted_iota(jnp.int32, (wide, LANES), 1)
    column = lane - jnp.where(lane >= WIN, WIN, 0) - jnp.where(lane >= 2 * WIN, WIN, 0)
    pick = (spot == LANES - HALO + STRIP * strip + column) & (lane < VARS * WIN)
    cls_out_ref[...] = jnp.dot(wide_ref[...], pick.astype(F32).astype(BF16), preferred_element_type=F32)


def patch_kernel(side_ref, inner_ref, cls_ref, out_ref, cls_out_ref):
    first = lax.axis_index("col") == 0
    strip = lax.axis_index("member") // LEV
    end = COLS // STRIP - 1
    for l in range(LEV):
        side = side_ref[l * 2 * ROWS : (l + 1) * 2 * ROWS].astype(F32)
        for s, here in ((0, jnp.logical_not(first)), (end, first)):
            at = s * LEV + l
            out_ref[at] = (inner_ref[at].astype(F32) + jnp.where(here, side, 0.0)).astype(BF16)
    mine = strip == jnp.where(first, end, 0)
    cls_out_ref[...] = cls_ref[...] + jnp.where(mine, side_ref[LEV * 2 * ROWS :].astype(F32), 0.0)


def edge_kernel(got_ref, cls_ref, up_ref, dn_ref):
    members = got_ref.shape[0]
    up_ref[:members] = got_ref[:, :8]
    dn_ref[:members] = got_ref[:, 8:16]
    up_ref[members] = cls_ref[:8].astype(BF16)
    dn_ref[members] = pltpu.roll(cls_ref[8:], HALO, 0).astype(BF16)


TOP = 8
TALL = TOP + ROWS + TOP
FORWARD = [
    (dy, dx)
    for dy in range(HALO + 1)
    for dx in range(-HALO, HALO + 1)
    if dy + abs(dx) <= HALO and (dy > 0 or dx >= 0)
]
EVERY = [(dy, dx) for dx in range(-HALO, HALO + 1) for dy in range(-HALO, HALO + 1) if abs(dy) + abs(dx) <= HALO]
AT = {d: i for i, d in enumerate(EVERY)}


def lanes_by(x, dx):
    return pltpu.roll(x, (-dx) % LANES, 1) if dx else x


def rates_of(cls, rates_ref):
    rate = jnp.zeros(cls.shape, F32)
    for k in range(rates_ref.shape[0]):
        rate = jnp.where(cls == float(k + 1), rates_ref[k : k + 1], rate)
    return rate


def entries(rows_at):
    steps = ((0, 1), (0, -1), (1, 0), (-1, 0))
    near = {dy: rows_at(dy) for dy in range(-HALO + 1, HALO)}
    at = {(dy, dx): lanes_by(near[dy], dx) for dy, dx in EVERY if abs(dy) + abs(dx) < HALO}
    coef = {(0, 0): 1.0 - 4.0 * at[(0, 0)]}
    for e in steps:
        coef[e] = at[(0, 0)]
    for sweep in range(1, SWEEPS):
        flow = {d: c * at[d] for d, c in coef.items()}
        to = {(d[0] + e[0], d[1] + e[1]) for d in flow for e in steps}
        new = {}
        for d in EVERY:
            if d not in to:
                continue
            terms = [flow[(d[0] - e[0], d[1] - e[1])] for e in steps if (d[0] - e[0], d[1] - e[1]) in flow]
            if d in coef:
                terms.append(coef[d] - 4.0 * flow[d])
            total = terms[0]
            for t in terms[1:]:
                total = total + t
            new[d] = total
        coef = new
    return coef


def set_weights(weight_ref, coef, gram_at, scale):
    for i, (dy, dx) in enumerate(FORWARD):
        weight_ref[AT[(dy, dx)]] = lanes_by(coef[(dy, dx)] * scale * gram_at(i, dy), -dx)
        if (dy, dx) != (0, 0):
            weight_ref[AT[(-dy, -dx)]] = lanes_by(coef[(-dy, -dx)] * scale, dx) * gram_at(i, 0)


def weighted(weight_ref, rows):
    total = None
    for dx in range(-HALO, HALO + 1):
        part = None
        for dy in range(-HALO + abs(dx), HALO - abs(dx) + 1):
            term = weight_ref[AT[(dy, dx)]] * rows[dy + HALO]
            part = term if part is None else part + term
        part = lanes_by(part, dx)
        total = part if total is None else total + part
    return total


def own_kernel(rates_ref, got_ref, cls_ref, gram_ref, prob_ref, mid_ref, pert_ref, weight_ref, rate_ref):
    members = got_ref.shape[0]
    blank = jnp.zeros((TOP, LANES), F32)

    def spread(m, _):
        tile = got_ref[m].astype(F32)
        pert_ref[m, 0:TOP] = blank
        for group, to in enumerate((0, 12, 4, 8)):
            pert_ref[m, TOP + to : TOP + to + HALO] = tile[8 * group : 8 * group + HALO]
            prob_ref[m, TOP + to : TOP + to + HALO] = tile[8 * group + HALO : 8 * group + 8]
        return 0

    lax.fori_loop(0, members, spread, 0, unroll=4)
    for b in range(2):
        row = TOP + 8 * b

        def products(m, acc):
            low = pert_ref[m, row : row + 8]
            high = [pert_ref[m, row - dy : row - dy + 8] for dy in range(HALO + 1)]
            near = {dx: lanes_by(low, dx) for dx in range(-HALO + 1, HALO + 1)}
            return tuple(a + high[dy] * near[dx] for a, (dy, dx) in zip(acc, FORWARD))

        acc = tuple(jnp.zeros((8, LANES), F32) for _ in FORWARD)
        acc = lax.fori_loop(0, members, products, acc, unroll=4)
        for i, a in enumerate(acc):
            gram_ref[i, 8 * b : 8 * b + 8] = a

    rate_ref[...] = rates_of(cls_ref[...], rates_ref)
    coef = entries(lambda dy: rate_ref[HALO + dy : HALO + dy + 8])
    set_weights(weight_ref, coef, lambda i, dy: gram_ref[i, HALO + dy : HALO + dy + 8], 1.0 / (members - 1))

    def one_probe(p, _):
        start = TOP + HALO
        mid_ref[p] = weighted(weight_ref, [prob_ref[p, start + dy : start + dy + 8] for dy in range(-HALO, HALO + 1)])
        return 0

    lax.fori_loop(0, members, one_probe, 0, unroll=8)


def apply_kernel(
    n_row, rates_ref, got_ref, cls_ref, below_ref, above_ref, own_ref, mid_ref, part_ref, out_ref,
    prob_ref, gram_ref, weight_ref, rate_ref,
):
    members = got_ref.shape[0]
    has_below = lax.axis_index("row") != n_row - 1
    has_above = lax.axis_index("row") != 0
    blank = jnp.zeros((HALO, LANES), F32)
    sub = lax.broadcasted_iota(jnp.int32, (8, LANES), 0)
    lane = lax.broadcasted_iota(jnp.int32, (8, LANES), 1)
    upper = sub < HALO
    crossing = [d for d in FORWARD if d[0] > 0]

    def spread(m, acc):
        tile = got_ref[m, :ROWS].astype(F32)
        below, above = below_ref[m].astype(F32), above_ref[m].astype(F32)
        prob_ref[m, TOP - HALO : TOP] = above[HALO:]
        prob_ref[m, TOP + ROWS : TOP + ROWS + HALO] = below[HALO:]
        low = jnp.where(upper, tile[0:8], pltpu.roll(below, HALO, 0))
        high = jnp.where(upper, above, pltpu.roll(tile[8:16], HALO, 0))
        high = {dy: pltpu.roll(high, HALO + dy, 0) if dy < HALO else high for dy in range(1, HALO + 1)}
        near = {dx: lanes_by(low, dx) for dx in range(-HALO + 1, HALO)}
        return tuple(a + high[dy] * near[dx] for a, (dy, dx) in zip(acc, crossing))

    acc = tuple(jnp.zeros((8, LANES), F32) for _ in crossing)
    acc = lax.fori_loop(0, members, spread, acc, unroll=4)
    inside = (upper & has_above) | (jnp.logical_not(upper) & has_below)
    acc = {d: jnp.where(inside, a, 0.0) for d, a in zip(crossing, acc)}
    for i, d in enumerate(FORWARD):
        gram_ref[i, 8:16] = own_ref[i, 8:16]
        if d in acc:
            gram_ref[i, 0:8] = own_ref[i, 0:8] + jnp.where(sub < d[0], acc[d], 0.0)
            gram_ref[i, 16:24] = pltpu.roll(acc[d], HALO, 0)
        else:
            gram_ref[i, 0:8] = own_ref[i, 0:8]

    cls = jnp.concatenate(
        [
            blank,
            jnp.where(has_above, above_ref[members, :HALO].astype(F32), 0.0),
            cls_ref[...],
            jnp.where(has_below, below_ref[members, :HALO].astype(F32), 0.0),
            blank,
        ],
        axis=0,
    )
    rate_ref[...] = rates_of(cls, rates_ref)
    coef = entries(
        lambda dy: jnp.where(upper, rate_ref[TOP + dy : TOP + dy + 8], rate_ref[TOP + 8 + dy : TOP + dy + 16])
    )
    set_weights(
        weight_ref,
        coef,
        lambda i, dy: jnp.where(upper, gram_ref[i, dy : dy + 8], gram_ref[i, 8 + dy : dy + 16]),
        1.0 / (members - 1),
    )

    turn = lax.axis_index("member") // LEV % (LANES // STRIP) * STRIP
    slot = (lane - turn) & (LANES - 1)

    def turned(x, dx):
        return pltpu.roll(x, (turn + (-dx) % LANES) & (LANES - 1), 1)

    def one_probe(p, _):
        rows = [
            jnp.where(upper, prob_ref[p, TOP + dy : TOP + dy + 8], prob_ref[p, TOP + 8 + dy : TOP + dy + 16])
            for dy in range(-HALO, HALO + 1)
        ]
        a, b = weighted(weight_ref, rows), mid_ref[p]
        first = jnp.where(slot < STRIP, turned(a, HALO), turned(a, HALO + 8))
        first = jnp.where(slot < 2 * STRIP, first, turned(a, HALO + 16))
        first = jnp.where(slot < 3 * STRIP, first, turned(b, HALO - 3 * STRIP))
        rest = jnp.where(slot < STRIP, turned(b, WIN + HALO), turned(b, 2 * WIN + HALO - STRIP))
        rest = jnp.where(slot < 2 * STRIP, rest, pltpu.roll(lanes_by(rest, 2 * STRIP), HALO, 0))
        out_ref[p, 0] = first[:HALO]
        out_ref[p, 1] = first[HALO:]
        out_ref[p, 2] = rest[:HALO]
        return 0

    lax.fori_loop(0, members, one_probe, 0, unroll=8)


def unpack_kernel(got_ref, out_ref, tile_ref, sems):
    per = LANES // STRIP
    blocks = COLS // LANES
    slots = [lax.broadcasted_iota(jnp.int32, (rows, LANES), 1) // STRIP for rows in (HALO, 8)]

    def joined(parts, first):
        slot = slots[0] if parts[0].shape[0] == HALO else slots[1]
        acc = parts[0]
        for q in range(1, per):
            acc = jnp.where(slot == (first + q) % per, parts[q], acc)
        return pltpu.roll(acc, (-first * STRIP) % LANES, 1) if first % per else acc

    copies = []
    for l in range(LEV):
        for at in range(blocks):
            got = [got_ref[(at * per + q) * LEV + l] for q in range(per)]
            top = [jnp.concatenate([g[0], g[1]], axis=0) for g in got]
            low = [g[2] for g in got]
            span = slice(at * LANES, (at + 1) * LANES)
            for v in range(VARS):
                ends = joined(top, v)
                tile_ref[v, l, :HALO, span] = ends[:HALO]
                tile_ref[v, l, ROWS - HALO :, span] = ends[HALO:]
                if v == 0:
                    tile_ref[v, l, HALO : HALO + 8, span] = joined(top, VARS)
                else:
                    tile_ref[v, l, HALO : 2 * HALO, span] = joined(low, v - 1)
                    tile_ref[v, l, 2 * HALO : 3 * HALO, span] = joined(low, v + 1)
        for v in range(VARS):
            copy = pltpu.make_async_copy(tile_ref.at[v, l], out_ref.at[0, v, l], sems.at[v * LEV + l])
            copy.start()
            copies.append(copy)
    for copy in copies:
        copy.wait()


def body(pert, probes, diff_class, class_rate):
    members = lax.axis_size("member")
    n_row = lax.axis_size("row")
    vmem = pl.BlockSpec(memory_space=pltpu.VMEM)
    smem = pl.BlockSpec(memory_space=pltpu.SMEM)
    shape = pltpu.VMEM

    def near(x):
        return pltpu.with_memory_space_constraint(x, pltpu.VMEM)

    ends = (0, COLS // LANES - 1)
    tile = [pl.BlockSpec((1, VARS, LEV, ROWS, LANES), functools.partial(lambda at, i: (0, 0, 0, 0, at), at)) for at in ends]
    plane = [pl.BlockSpec((ROWS, LANES), functools.partial(lambda at, i: (0, at), at)) for at in ends]
    side = pl.pallas_call(
        side_kernel,
        grid=(1,),
        in_specs=tile + tile + plane,
        out_specs=vmem,
        out_shape=shape(((2 * LEV + 1) * ROWS, LANES), BF16),
        name="side",
    )(pert, pert, probes, probes, diff_class, diff_class)
    beside = lax.ppermute(side, "col", [(0, 1), (1, 0)])

    chunk, classes = shape((members, 2 * ROWS, LANES), BF16), shape((ROWS, LANES), F32)
    inner, cls, rates = pl.pallas_call(
        pack_kernel,
        in_specs=[smem] + [vmem] * 3,
        out_specs=[vmem] * 3,
        out_shape=[chunk, classes, shape((class_rate.shape[0], LANES), F32)],
        scratch_shapes=[pltpu.VMEM((ROWS, COLS + 2 * LANES), BF16)],
        name="pack",
    )(class_rate, pert, probes, diff_class)
    chunks, cls = pl.pallas_call(
        patch_kernel,
        in_specs=[vmem] * 3,
        out_specs=[vmem] * 2,
        out_shape=[chunk, classes],
        input_output_aliases={1: 0},
        name="patch",
    )(near(beside), near(inner), near(cls))

    got = lax.all_to_all(chunks, "member", 0, 0, tiled=True)

    edge = shape((members + 1, 8, LANES), BF16)
    up, dn = pl.pallas_call(
        edge_kernel,
        in_specs=[vmem] * 2,
        out_specs=[vmem] * 2,
        out_shape=[edge, edge],
        name="edges",
    )(near(got), near(cls))
    below = lax.ppermute(up, "row", [(i, (i - 1) % n_row) for i in range(n_row)])
    above = lax.ppermute(dn, "row", [(i, (i + 1) % n_row) for i in range(n_row)])

    tall = shape((members, TALL, LANES), F32)
    weights = pltpu.VMEM((len(EVERY), 8, LANES), F32)
    own, spread, mid = pl.pallas_call(
        own_kernel,
        in_specs=[vmem] * 3,
        out_specs=[vmem] * 3,
        out_shape=[shape((len(FORWARD), ROWS, LANES), F32), tall, shape((members, 8, LANES), F32)],
        scratch_shapes=[
            pltpu.VMEM((members, TOP + ROWS, LANES), F32),
            weights,
            pltpu.VMEM((ROWS, LANES), F32),
        ],
        name="own",
    )(near(rates), near(got), near(cls))

    part, spread = pl.pallas_call(
        functools.partial(apply_kernel, n_row),
        in_specs=[vmem] * 8,
        out_specs=[vmem] * 2,
        out_shape=[shape((members, VARS, HALO, LANES), F32), tall],
        input_output_aliases={7: 1},
        scratch_shapes=[
            pltpu.VMEM((len(FORWARD), 24, LANES), F32),
            weights,
            pltpu.VMEM((TALL, LANES), F32),
        ],
        name="apply",
    )(near(rates), near(got), near(cls), near(below), near(above), near(own), near(mid), near(spread))

    back = lax.all_to_all(part, "member", 0, 0, tiled=True)

    return pl.pallas_call(
        unpack_kernel,
        in_specs=[vmem],
        out_specs=pl.BlockSpec(memory_space=pl.ANY),
        out_shape=jax.ShapeDtypeStruct((1, VARS, LEV, ROWS, COLS), F32),
        scratch_shapes=[
            pltpu.VMEM((VARS, LEV, ROWS, COLS), F32),
            pltpu.SemaphoreType.DMA((VARS * LEV,)),
        ],
        name="unpack",
    )(near(back))


def solution(mesh):
    placed = (
        P("member", None, None, "row", "col"),
        P("member", None, None, "row", "col"),
        P("row", "col"),
        P(),
    )
    return jax.shard_map(
        body,
        mesh=mesh,
        in_specs=placed,
        out_specs=P("member", None, None, "row", "col"),
        check_vma=False,
    )
```

```python
import functools

import jax
import jax.numpy as jnp
from jax import lax
from jax.experimental import pallas as pl
from jax.experimental.pallas import tpu as pltpu
from jax.sharding import PartitionSpec as P

SWEEPS = 4
VARS = 3
LEV = 2
ROWS = 16
COLS = 512
HALO = 4
STRIP = 32
WIN = STRIP + 2 * HALO
LANES = 128
F32 = jnp.float32
BF16 = jnp.bfloat16


def grouped(a, b):
    upper = lax.broadcasted_iota(jnp.int32, (8, LANES), 0) < HALO
    groups = [
        jnp.where(upper, a[:8], pltpu.roll(b[:8], HALO, 0)),
        jnp.where(upper, pltpu.roll(a[8:], HALO, 0), b[8:]),
        jnp.where(upper, pltpu.roll(a[:8], HALO, 0), b[:8]),
        jnp.where(upper, a[8:], pltpu.roll(b[8:], HALO, 0)),
    ]
    return jnp.concatenate(groups, axis=0).astype(BF16)


def side_kernel(pert_ref, prob_ref, cls_ref, side_ref, pert_end, prob_end, cls_end, sems):
    last = lax.axis_index("col") == 0
    at = pl.ds(pl.multiple_of(jnp.where(last, COLS - LANES, 0), LANES), LANES)
    copies = [
        pltpu.make_async_copy(pert_ref.at[0, :, :, :, at], pert_end, sems.at[0]),
        pltpu.make_async_copy(prob_ref.at[0, :, :, :, at], prob_end, sems.at[1]),
        pltpu.make_async_copy(cls_ref.at[:, at], cls_end, sems.at[2]),
    ]
    for copy in copies:
        copy.start()
    lane = lax.broadcasted_iota(jnp.int32, (ROWS, LANES), 1)
    low = jnp.where(last, 0, WIN - HALO)
    use = [(lane >= WIN * v + low) & (lane < WIN * v + low + HALO) for v in range(VARS)]
    for copy in copies:
        copy.wait()

    def placed(planes):
        acc = jnp.zeros((ROWS, LANES), F32)
        for v, plane in enumerate(planes):
            shift = jnp.where(last, WIN * v + HALO, WIN * v + WIN - HALO)
            acc = jnp.where(use[v], pltpu.roll(plane, shift, 1), acc)
        return acc

    for l in range(LEV):
        a, b = (placed([end[v, l].astype(F32) for v in range(VARS)]) for end in (pert_end, prob_end))
        side_ref[l * 2 * ROWS : (l + 1) * 2 * ROWS] = grouped(a, b)
    side_ref[LEV * 2 * ROWS :] = placed([(cls_end[...] + 1).astype(F32)] * VARS).astype(BF16)


def pack_kernel(rates_ref, pert_ref, prob_ref, cls_ref, out_ref, cls_out_ref, rates_out_ref, wide_ref):
    lane = lax.broadcasted_iota(jnp.int32, (ROWS, LANES), 1)
    blocks = COLS // LANES
    for k in range(rates_ref.shape[0]):
        rates_out_ref[k : k + 1] = jnp.full((1, LANES), rates_ref[k], F32)

    def block(ref, v, l, at, shift):
        got = ref[0, v, l, :, at * LANES : (at + 1) * LANES].astype(F32)
        return pltpu.roll(got, shift, 1) if shift else got

    for s in range(COLS // STRIP):
        start = s * STRIP - HALO
        at, off = start // LANES, start % LANES
        for l in range(LEV):
            both = []
            for ref in (pert_ref, prob_ref):
                acc = jnp.zeros((ROWS, LANES), F32)
                for v in range(VARS):
                    shift = (WIN * v - off) % LANES
                    low, high = WIN * v, WIN * (v + 1)
                    split = low + LANES - off
                    if at >= 0:
                        use = (lane >= low) & (lane < min(high, split))
                        acc = jnp.where(use, block(ref, v, l, at, shift), acc)
                    if split < high and at + 1 < blocks:
                        use = (lane >= split) & (lane < high)
                        acc = jnp.where(use, block(ref, v, l, at + 1, shift), acc)
                both.append(acc)
            out_ref[s * LEV + l] = grouped(*both)

    zero = jnp.zeros((ROWS, LANES), BF16)
    wide_ref[:, :LANES] = zero
    wide_ref[:, LANES : LANES + COLS] = (cls_ref[...] + 1).astype(F32).astype(BF16)
    wide_ref[:, LANES + COLS :] = zero
    strip = lax.axis_index("member") // LEV
    wide = wide_ref.shape[1]
    spot = lax.broadcasted_iota(jnp.int32, (wide, LANES), 0)
    lane = lax.broadcasted_iota(jnp.int32, (wide, LANES), 1)
    column = lane - jnp.where(lane >= WIN, WIN, 0) - jnp.where(lane >= 2 * WIN, WIN, 0)
    pick = (spot == LANES - HALO + STRIP * strip + column) & (lane < VARS * WIN)
    cls_out_ref[...] = jnp.dot(wide_ref[...], pick.astype(F32).astype(BF16), preferred_element_type=F32)


def patch_kernel(side_ref, inner_ref, cls_ref, out_ref, cls_out_ref):
    first = lax.axis_index("col") == 0
    strip = lax.axis_index("member") // LEV
    end = COLS // STRIP - 1
    for l in range(LEV):
        side = side_ref[l * 2 * ROWS : (l + 1) * 2 * ROWS].astype(F32)
        for s, here in ((0, jnp.logical_not(first)), (end, first)):
            at = s * LEV + l
            out_ref[at] = (inner_ref[at].astype(F32) + jnp.where(here, side, 0.0)).astype(BF16)
    mine = strip == jnp.where(first, end, 0)
    cls_out_ref[...] = cls_ref[...] + jnp.where(mine, side_ref[LEV * 2 * ROWS :].astype(F32), 0.0)


def edge_kernel(got_ref, cls_ref, up_ref, dn_ref):
    members = got_ref.shape[0]
    up_ref[:members] = got_ref[:, :8]
    dn_ref[:members] = got_ref[:, 8:16]
    up_ref[members] = cls_ref[:8].astype(BF16)
    dn_ref[members] = pltpu.roll(cls_ref[8:], HALO, 0).astype(BF16)


TOP = 8
TALL = TOP + ROWS + TOP
FORWARD = [
    (dy, dx)
    for dy in range(HALO + 1)
    for dx in range(-HALO, HALO + 1)
    if dy + abs(dx) <= HALO and (dy > 0 or dx >= 0)
]
EVERY = [(dy, dx) for dx in range(-HALO, HALO + 1) for dy in range(-HALO, HALO + 1) if abs(dy) + abs(dx) <= HALO]
AT = {d: i for i, d in enumerate(EVERY)}


def lanes_by(x, dx):
    return pltpu.roll(x, (-dx) % LANES, 1) if dx else x


def rates_of(cls, rates_ref):
    rate = jnp.zeros(cls.shape, F32)
    for k in range(rates_ref.shape[0]):
        rate = jnp.where(cls == float(k + 1), rates_ref[k : k + 1], rate)
    return rate


def entries(rows_at):
    steps = ((0, 1), (0, -1), (1, 0), (-1, 0))
    near = {dy: rows_at(dy) for dy in range(-HALO + 1, HALO)}
    at = {(dy, dx): lanes_by(near[dy], dx) for dy, dx in EVERY if abs(dy) + abs(dx) < HALO}
    coef = {(0, 0): 1.0 - 4.0 * at[(0, 0)]}
    for e in steps:
        coef[e] = at[(0, 0)]
    for sweep in range(1, SWEEPS):
        flow = {d: c * at[d] for d, c in coef.items()}
        to = {(d[0] + e[0], d[1] + e[1]) for d in flow for e in steps}
        new = {}
        for d in EVERY:
            if d not in to:
                continue
            terms = [flow[(d[0] - e[0], d[1] - e[1])] for e in steps if (d[0] - e[0], d[1] - e[1]) in flow]
            if d in coef:
                terms.append(coef[d] - 4.0 * flow[d])
            total = terms[0]
            for t in terms[1:]:
                total = total + t
            new[d] = total
        coef = new
    return coef


def set_weights(weight_ref, coef, gram_at, scale):
    for i, (dy, dx) in enumerate(FORWARD):
        weight_ref[AT[(dy, dx)]] = lanes_by(coef[(dy, dx)] * scale * gram_at(i, dy), -dx)
        if (dy, dx) != (0, 0):
            weight_ref[AT[(-dy, -dx)]] = lanes_by(coef[(-dy, -dx)] * scale, dx) * gram_at(i, 0)


def weighted(weight_ref, rows):
    total = None
    for dx in range(-HALO, HALO + 1):
        part = None
        for dy in range(-HALO + abs(dx), HALO - abs(dx) + 1):
            term = weight_ref[AT[(dy, dx)]] * rows[dy + HALO]
            part = term if part is None else part + term
        part = lanes_by(part, dx)
        total = part if total is None else total + part
    return total


def turning(rows):
    turn = lax.axis_index("member") // LEV % (LANES // STRIP) * STRIP
    slot = (lax.broadcasted_iota(jnp.int32, (rows, LANES), 1) - turn) & (LANES - 1)

    def turned(x, dx):
        return pltpu.roll(x, (turn + (-dx) % LANES) & (LANES - 1), 1)

    return slot, turned


def own_kernel(rates_ref, got_ref, cls_ref, gram_ref, prob_ref, mid_ref, out_ref, pert_ref, weight_ref, rate_ref):
    members = got_ref.shape[0]
    blank = jnp.zeros((TOP, LANES), F32)

    def spread(m, _):
        tile = got_ref[m].astype(F32)
        pert_ref[m, 0:TOP] = blank
        for group, to in enumerate((0, 12, 4, 8)):
            pert_ref[m, TOP + to : TOP + to + HALO] = tile[8 * group : 8 * group + HALO]
            prob_ref[m, TOP + to : TOP + to + HALO] = tile[8 * group + HALO : 8 * group + 8]
        return 0

    lax.fori_loop(0, members, spread, 0, unroll=4)
    for b in range(2):
        row = TOP + 8 * b

        def products(m, acc):
            low = pert_ref[m, row : row + 8]
            high = [pert_ref[m, row - dy : row - dy + 8] for dy in range(HALO + 1)]
            near = {dx: lanes_by(low, dx) for dx in range(-HALO + 1, HALO + 1)}
            return tuple(a + high[dy] * near[dx] for a, (dy, dx) in zip(acc, FORWARD))

        acc = tuple(jnp.zeros((8, LANES), F32) for _ in FORWARD)
        acc = lax.fori_loop(0, members, products, acc, unroll=16)
        for i, a in enumerate(acc):
            gram_ref[i, 8 * b : 8 * b + 8] = a

    rate_ref[...] = rates_of(cls_ref[...], rates_ref)
    coef = entries(lambda dy: rate_ref[HALO + dy : HALO + dy + 8])
    set_weights(weight_ref, coef, lambda i, dy: gram_ref[i, HALO + dy : HALO + dy + 8], 1.0 / (members - 1))

    slot, turned = turning(8)

    def one_probe(p, _):
        start = TOP + HALO
        b = weighted(weight_ref, [prob_ref[p, start + dy : start + dy + 8] for dy in range(-HALO, HALO + 1)])
        mid_ref[p] = turned(b, HALO - 3 * STRIP)
        rest = jnp.where(slot < STRIP, turned(b, WIN + HALO), turned(b, 2 * WIN + HALO - STRIP))
        rest = jnp.where(slot < 2 * STRIP, rest, pltpu.roll(lanes_by(rest, 2 * STRIP), HALO, 0))
        out_ref[p, 2] = rest[:HALO]
        return 0

    lax.fori_loop(0, members, one_probe, 0, unroll=16)


def apply_kernel(
    n_row, rates_ref, got_ref, cls_ref, below_ref, above_ref, own_ref, mid_ref, part_ref, third_ref, out_ref,
    prob_ref, gram_ref, weight_ref, rate_ref,
):
    members = got_ref.shape[0]
    has_below = lax.axis_index("row") != n_row - 1
    has_above = lax.axis_index("row") != 0
    blank = jnp.zeros((HALO, LANES), F32)
    sub = lax.broadcasted_iota(jnp.int32, (8, LANES), 0)
    upper = sub < HALO
    crossing = [d for d in FORWARD if d[0] > 0]

    def spread(m, acc):
        tile = got_ref[m, :ROWS].astype(F32)
        below, above = below_ref[m].astype(F32), above_ref[m].astype(F32)
        prob_ref[m, TOP - HALO : TOP] = above[HALO:]
        prob_ref[m, TOP + ROWS : TOP + ROWS + HALO] = below[HALO:]
        low = jnp.where(upper, tile[0:8], pltpu.roll(below, HALO, 0))
        high = jnp.where(upper, above, pltpu.roll(tile[8:16], HALO, 0))
        high = {dy: pltpu.roll(high, HALO + dy, 0) if dy < HALO else high for dy in range(1, HALO + 1)}
        near = {dx: lanes_by(low, dx) for dx in range(-HALO + 1, HALO)}
        return tuple(a + high[dy] * near[dx] for a, (dy, dx) in zip(acc, crossing))

    acc = tuple(jnp.zeros((8, LANES), F32) for _ in crossing)
    acc = lax.fori_loop(0, members, spread, acc, unroll=4)
    inside = (upper & has_above) | (jnp.logical_not(upper) & has_below)
    acc = {d: jnp.where(inside, a, 0.0) for d, a in zip(crossing, acc)}
    for i, d in enumerate(FORWARD):
        gram_ref[i, 8:16] = own_ref[i, 8:16]
        if d in acc:
            gram_ref[i, 0:8] = own_ref[i, 0:8] + jnp.where(sub < d[0], acc[d], 0.0)
            gram_ref[i, 16:24] = pltpu.roll(acc[d], HALO, 0)
        else:
            gram_ref[i, 0:8] = own_ref[i, 0:8]

    cls = jnp.concatenate(
        [
            blank,
            jnp.where(has_above, above_ref[members, :HALO].astype(F32), 0.0),
            cls_ref[...],
            jnp.where(has_below, below_ref[members, :HALO].astype(F32), 0.0),
            blank,
        ],
        axis=0,
    )
    rate_ref[...] = rates_of(cls, rates_ref)
    coef = entries(
        lambda dy: jnp.where(upper, rate_ref[TOP + dy : TOP + dy + 8], rate_ref[TOP + 8 + dy : TOP + dy + 16])
    )
    set_weights(
        weight_ref,
        coef,
        lambda i, dy: jnp.where(upper, gram_ref[i, dy : dy + 8], gram_ref[i, 8 + dy : dy + 16]),
        1.0 / (members - 1),
    )

    slot, turned = turning(8)

    def one_probe(p, _):
        rows = [
            jnp.where(upper, prob_ref[p, TOP + dy : TOP + dy + 8], prob_ref[p, TOP + 8 + dy : TOP + dy + 16])
            for dy in range(-HALO, HALO + 1)
        ]
        a = weighted(weight_ref, rows)
        first = jnp.where(slot < STRIP, turned(a, HALO), turned(a, HALO + 8))
        first = jnp.where(slot < 2 * STRIP, first, turned(a, HALO + 16))
        first = jnp.where(slot < 3 * STRIP, first, mid_ref[p])
        out_ref[p, 0] = first[:HALO]
        out_ref[p, 1] = first[HALO:]
        return 0

    lax.fori_loop(0, members, one_probe, 0, unroll=8)


def unpack_kernel(got_ref, out_ref, tile_ref, sems):
    per = LANES // STRIP
    blocks = COLS // LANES
    slots = [lax.broadcasted_iota(jnp.int32, (rows, LANES), 1) // STRIP for rows in (HALO, 8)]

    def joined(parts, first):
        slot = slots[0] if parts[0].shape[0] == HALO else slots[1]
        acc = parts[0]
        for q in range(1, per):
            acc = jnp.where(slot == (first + q) % per, parts[q], acc)
        return pltpu.roll(acc, (-first * STRIP) % LANES, 1) if first % per else acc

    copies = []
    for l in range(LEV):
        for at in range(blocks):
            got = [got_ref[(at * per + q) * LEV + l] for q in range(per)]
            top = [jnp.concatenate([g[0], g[1]], axis=0) for g in got]
            low = [g[2] for g in got]
            span = slice(at * LANES, (at + 1) * LANES)
            for v in range(VARS):
                ends = joined(top, v)
                tile_ref[v, l, :HALO, span] = ends[:HALO]
                tile_ref[v, l, ROWS - HALO :, span] = ends[HALO:]
                if v == 0:
                    tile_ref[v, l, HALO : HALO + 8, span] = joined(top, VARS)
                else:
                    tile_ref[v, l, HALO : 2 * HALO, span] = joined(low, v - 1)
                    tile_ref[v, l, 2 * HALO : 3 * HALO, span] = joined(low, v + 1)
        for v in range(VARS):
            copy = pltpu.make_async_copy(tile_ref.at[v, l], out_ref.at[0, v, l], sems.at[v * LEV + l])
            copy.start()
            copies.append(copy)
    for copy in copies:
        copy.wait()


def body(pert, probes, diff_class, class_rate):
    members = lax.axis_size("member")
    n_row = lax.axis_size("row")
    vmem = pl.BlockSpec(memory_space=pltpu.VMEM)
    smem = pl.BlockSpec(memory_space=pltpu.SMEM)
    shape = pltpu.VMEM

    def near(x):
        return pltpu.with_memory_space_constraint(x, pltpu.VMEM)

    end = pltpu.VMEM((VARS, LEV, ROWS, LANES), BF16)
    side = pl.pallas_call(
        side_kernel,
        in_specs=[pl.BlockSpec(memory_space=pl.ANY)] * 3,
        out_specs=vmem,
        out_shape=shape(((2 * LEV + 1) * ROWS, LANES), BF16),
        scratch_shapes=[end, end, pltpu.VMEM((ROWS, LANES), jnp.int32), pltpu.SemaphoreType.DMA((3,))],
        name="side",
    )(pert, probes, diff_class)
    beside = lax.ppermute(side, "col", [(0, 1), (1, 0)])

    chunk, classes = shape((members, 2 * ROWS, LANES), BF16), shape((ROWS, LANES), F32)
    inner, cls, rates = pl.pallas_call(
        pack_kernel,
        in_specs=[smem] + [vmem] * 3,
        out_specs=[vmem] * 3,
        out_shape=[chunk, classes, shape((class_rate.shape[0], LANES), F32)],
        scratch_shapes=[pltpu.VMEM((ROWS, COLS + 2 * LANES), BF16)],
        name="pack",
    )(class_rate, pert, probes, diff_class)
    chunks, cls = pl.pallas_call(
        patch_kernel,
        in_specs=[vmem] * 3,
        out_specs=[vmem] * 2,
        out_shape=[chunk, classes],
        input_output_aliases={1: 0},
        name="patch",
    )(near(beside), near(inner), near(cls))

    got = lax.all_to_all(chunks, "member", 0, 0, tiled=True)

    edge = shape((members + 1, 8, LANES), BF16)
    up, dn = pl.pallas_call(
        edge_kernel,
        in_specs=[vmem] * 2,
        out_specs=[vmem] * 2,
        out_shape=[edge, edge],
        name="edges",
    )(near(got), near(cls))
    below = lax.ppermute(up, "row", [(i, (i - 1) % n_row) for i in range(n_row)])
    above = lax.ppermute(dn, "row", [(i, (i + 1) % n_row) for i in range(n_row)])

    tall = shape((members, TALL, LANES), F32)
    weights = pltpu.VMEM((len(EVERY), 8, LANES), F32)
    third = shape((members, VARS, HALO, LANES), F32)
    own, spread, mid, part = pl.pallas_call(
        own_kernel,
        in_specs=[vmem] * 3,
        out_specs=[vmem] * 4,
        out_shape=[shape((len(FORWARD), ROWS, LANES), F32), tall, shape((members, 8, LANES), F32), third],
        scratch_shapes=[
            pltpu.VMEM((members, TOP + ROWS, LANES), F32),
            weights,
            pltpu.VMEM((ROWS, LANES), F32),
        ],
        name="own",
    )(near(rates), near(got), near(cls))

    part, spread = pl.pallas_call(
        functools.partial(apply_kernel, n_row),
        in_specs=[vmem] * 9,
        out_specs=[vmem] * 2,
        out_shape=[third, tall],
        input_output_aliases={7: 1, 8: 0},
        scratch_shapes=[
            pltpu.VMEM((len(FORWARD), 24, LANES), F32),
            weights,
            pltpu.VMEM((TALL, LANES), F32),
        ],
        name="apply",
    )(near(rates), near(got), near(cls), near(below), near(above), near(own), near(mid), near(spread), near(part))

    back = lax.all_to_all(part, "member", 0, 0, tiled=True)

    return pl.pallas_call(
        unpack_kernel,
        in_specs=[vmem],
        out_specs=pl.BlockSpec(memory_space=pl.ANY),
        out_shape=jax.ShapeDtypeStruct((1, VARS, LEV, ROWS, COLS), F32),
        scratch_shapes=[
            pltpu.VMEM((VARS, LEV, ROWS, COLS), F32),
            pltpu.SemaphoreType.DMA((VARS * LEV,)),
        ],
        name="unpack",
    )(near(back))


def solution(mesh):
    placed = (
        P("member", None, None, "row", "col"),
        P("member", None, None, "row", "col"),
        P("row", "col"),
        P(),
    )
    return jax.shard_map(
        body,
        mesh=mesh,
        in_specs=placed,
        out_specs=P("member", None, None, "row", "col"),
        check_vma=False,
    )
```

```python
import functools

import jax
import jax.numpy as jnp
from jax import lax
from jax.experimental import pallas as pl
from jax.experimental.pallas import tpu as pltpu
from jax.sharding import PartitionSpec as P

SWEEPS = 4
VARS = 3
LEV = 2
ROWS = 16
COLS = 512
HALO = 4
STRIP = 32
WIN = STRIP + 2 * HALO
LANES = 128
F32 = jnp.float32
BF16 = jnp.bfloat16


def grouped(a, b):
    upper = lax.broadcasted_iota(jnp.int32, (8, LANES), 0) < HALO
    groups = [
        jnp.where(upper, a[:8], pltpu.roll(b[:8], HALO, 0)),
        jnp.where(upper, pltpu.roll(a[8:], HALO, 0), b[8:]),
        jnp.where(upper, pltpu.roll(a[:8], HALO, 0), b[:8]),
        jnp.where(upper, a[8:], pltpu.roll(b[8:], HALO, 0)),
    ]
    return jnp.concatenate(groups, axis=0).astype(BF16)


def side_kernel(pert_ref, prob_ref, cls_ref, side_ref, pert_end, prob_end, cls_end, sems):
    last = lax.axis_index("col") == 0
    at = pl.ds(pl.multiple_of(jnp.where(last, COLS - LANES, 0), LANES), LANES)
    copies = [
        pltpu.make_async_copy(pert_ref.at[0, :, :, :, at], pert_end, sems.at[0]),
        pltpu.make_async_copy(prob_ref.at[0, :, :, :, at], prob_end, sems.at[1]),
        pltpu.make_async_copy(cls_ref.at[:, at], cls_end, sems.at[2]),
    ]
    for copy in copies:
        copy.start()
    lane = lax.broadcasted_iota(jnp.int32, (ROWS, LANES), 1)
    low = jnp.where(last, 0, WIN - HALO)
    use = [(lane >= WIN * v + low) & (lane < WIN * v + low + HALO) for v in range(VARS)]
    for copy in copies:
        copy.wait()

    def placed(planes):
        acc = jnp.zeros((ROWS, LANES), F32)
        for v, plane in enumerate(planes):
            shift = jnp.where(last, WIN * v + HALO, WIN * v + WIN - HALO)
            acc = jnp.where(use[v], pltpu.roll(plane, shift, 1), acc)
        return acc

    for l in range(LEV):
        a, b = (placed([end[v, l].astype(F32) for v in range(VARS)]) for end in (pert_end, prob_end))
        side_ref[l * 2 * ROWS : (l + 1) * 2 * ROWS] = grouped(a, b)
    side_ref[LEV * 2 * ROWS :] = placed([(cls_end[...] + 1).astype(F32)] * VARS).astype(BF16)


def pack_kernel(rates_ref, pert_ref, prob_ref, cls_ref, out_ref, cls_out_ref, rates_out_ref, wide_ref):
    lane = lax.broadcasted_iota(jnp.int32, (ROWS, LANES), 1)
    blocks = COLS // LANES
    for k in range(rates_ref.shape[0]):
        rates_out_ref[k : k + 1] = jnp.full((1, LANES), rates_ref[k], F32)

    def block(ref, v, l, at, shift):
        got = ref[0, v, l, :, at * LANES : (at + 1) * LANES].astype(F32)
        return pltpu.roll(got, shift, 1) if shift else got

    for s in range(COLS // STRIP):
        start = s * STRIP - HALO
        at, off = start // LANES, start % LANES
        for l in range(LEV):
            both = []
            for ref in (pert_ref, prob_ref):
                acc = jnp.zeros((ROWS, LANES), F32)
                for v in range(VARS):
                    shift = (WIN * v - off) % LANES
                    low, high = WIN * v, WIN * (v + 1)
                    split = low + LANES - off
                    if at >= 0:
                        use = (lane >= low) & (lane < min(high, split))
                        acc = jnp.where(use, block(ref, v, l, at, shift), acc)
                    if split < high and at + 1 < blocks:
                        use = (lane >= split) & (lane < high)
                        acc = jnp.where(use, block(ref, v, l, at + 1, shift), acc)
                both.append(acc)
            out_ref[s * LEV + l] = grouped(*both)

    zero = jnp.zeros((ROWS, LANES), BF16)
    wide_ref[:, :LANES] = zero
    wide_ref[:, LANES : LANES + COLS] = (cls_ref[...] + 1).astype(F32).astype(BF16)
    wide_ref[:, LANES + COLS :] = zero
    strip = lax.axis_index("member") // LEV
    wide = wide_ref.shape[1]
    spot = lax.broadcasted_iota(jnp.int32, (wide, LANES), 0)
    lane = lax.broadcasted_iota(jnp.int32, (wide, LANES), 1)
    column = lane - jnp.where(lane >= WIN, WIN, 0) - jnp.where(lane >= 2 * WIN, WIN, 0)
    pick = (spot == LANES - HALO + STRIP * strip + column) & (lane < VARS * WIN)
    cls_out_ref[...] = jnp.dot(wide_ref[...], pick.astype(F32).astype(BF16), preferred_element_type=F32)


def patch_kernel(side_ref, inner_ref, cls_ref, out_ref, cls_out_ref):
    first = lax.axis_index("col") == 0
    strip = lax.axis_index("member") // LEV
    end = COLS // STRIP - 1
    for l in range(LEV):
        side = side_ref[l * 2 * ROWS : (l + 1) * 2 * ROWS].astype(F32)
        for s, here in ((0, jnp.logical_not(first)), (end, first)):
            at = s * LEV + l
            out_ref[at] = (inner_ref[at].astype(F32) + jnp.where(here, side, 0.0)).astype(BF16)
    mine = strip == jnp.where(first, end, 0)
    cls_out_ref[...] = cls_ref[...] + jnp.where(mine, side_ref[LEV * 2 * ROWS :].astype(F32), 0.0)


def edge_kernel(got_ref, cls_ref, up_ref, dn_ref):
    members = got_ref.shape[0]
    up_ref[:members] = got_ref[:, :8]
    dn_ref[:members] = got_ref[:, 8:16]
    up_ref[members] = cls_ref[:8].astype(BF16)
    dn_ref[members] = pltpu.roll(cls_ref[8:], HALO, 0).astype(BF16)


TOP = 8
TALL = TOP + ROWS + TOP
FORWARD = [
    (dy, dx)
    for dy in range(HALO + 1)
    for dx in range(-HALO, HALO + 1)
    if dy + abs(dx) <= HALO and (dy > 0 or dx >= 0)
]
EVERY = [(dy, dx) for dx in range(-HALO, HALO + 1) for dy in range(-HALO, HALO + 1) if abs(dy) + abs(dx) <= HALO]
AT = {d: i for i, d in enumerate(EVERY)}


def lanes_by(x, dx):
    return pltpu.roll(x, (-dx) % LANES, 1) if dx else x


def rates_of(cls, rates_ref):
    rate = jnp.zeros(cls.shape, F32)
    for k in range(rates_ref.shape[0]):
        rate = jnp.where(cls == float(k + 1), rates_ref[k : k + 1], rate)
    return rate


def entries(rows_at):
    steps = ((0, 1), (0, -1), (1, 0), (-1, 0))
    near = {dy: rows_at(dy) for dy in range(-HALO + 1, HALO)}
    at = {(dy, dx): lanes_by(near[dy], dx) for dy, dx in EVERY if abs(dy) + abs(dx) < HALO}
    coef = {(0, 0): 1.0 - 4.0 * at[(0, 0)]}
    for e in steps:
        coef[e] = at[(0, 0)]
    for sweep in range(1, SWEEPS):
        flow = {d: c * at[d] for d, c in coef.items()}
        to = {(d[0] + e[0], d[1] + e[1]) for d in flow for e in steps}
        new = {}
        for d in EVERY:
            if d not in to:
                continue
            terms = [flow[(d[0] - e[0], d[1] - e[1])] for e in steps if (d[0] - e[0], d[1] - e[1]) in flow]
            if d in coef:
                terms.append(coef[d] - 4.0 * flow[d])
            total = terms[0]
            for t in terms[1:]:
                total = total + t
            new[d] = total
        coef = new
    return coef


def set_weights(weight_ref, coef, gram_at, scale):
    for i, (dy, dx) in enumerate(FORWARD):
        weight_ref[AT[(dy, dx)]] = lanes_by(coef[(dy, dx)] * scale * gram_at(i, dy), -dx)
        if (dy, dx) != (0, 0):
            weight_ref[AT[(-dy, -dx)]] = lanes_by(coef[(-dy, -dx)] * scale, dx) * gram_at(i, 0)


def weighted(weight_ref, rows):
    total = None
    for dx in range(-HALO, HALO + 1):
        part = None
        for dy in range(-HALO + abs(dx), HALO - abs(dx) + 1):
            term = weight_ref[AT[(dy, dx)]] * rows[dy + HALO]
            part = term if part is None else part + term
        part = lanes_by(part, dx)
        total = part if total is None else total + part
    return total


def turning(rows):
    turn = lax.axis_index("member") // LEV % (LANES // STRIP) * STRIP
    slot = (lax.broadcasted_iota(jnp.int32, (rows, LANES), 1) - turn) & (LANES - 1)

    def turned(x, dx):
        return pltpu.roll(x, (turn + (-dx) % LANES) & (LANES - 1), 1)

    return slot, turned


def own_kernel(
    rates_ref, got_ref, cls_ref, gram_ref, prob_ref, mid_ref, out_ref, ends_ref, pert_ref, weight_ref, rate_ref
):
    members = got_ref.shape[0]
    blank = jnp.zeros((TOP, LANES), F32)
    upper = lax.broadcasted_iota(jnp.int32, (8, LANES), 0) < HALO

    def spread(m, _):
        tile = got_ref[m].astype(F32)
        ends_ref[m] = jnp.where(upper, tile[0:8], pltpu.roll(tile[8:16], HALO, 0))
        pert_ref[m, 0:TOP] = blank
        for group, to in enumerate((0, 12, 4, 8)):
            pert_ref[m, TOP + to : TOP + to + HALO] = tile[8 * group : 8 * group + HALO]
            prob_ref[m, TOP + to : TOP + to + HALO] = tile[8 * group + HALO : 8 * group + 8]
        return 0

    lax.fori_loop(0, members, spread, 0, unroll=4)
    for b in range(2):
        row = TOP + 8 * b

        def products(m, acc):
            low = pert_ref[m, row : row + 8]
            high = [pert_ref[m, row - dy : row - dy + 8] for dy in range(HALO + 1)]
            near = {dx: lanes_by(low, dx) for dx in range(-HALO + 1, HALO + 1)}
            return tuple(a + high[dy] * near[dx] for a, (dy, dx) in zip(acc, FORWARD))

        acc = tuple(jnp.zeros((8, LANES), F32) for _ in FORWARD)
        acc = lax.fori_loop(0, members, products, acc, unroll=16)
        for i, a in enumerate(acc):
            gram_ref[i, 8 * b : 8 * b + 8] = a

    rate_ref[...] = rates_of(cls_ref[...], rates_ref)
    coef = entries(lambda dy: rate_ref[HALO + dy : HALO + dy + 8])
    set_weights(weight_ref, coef, lambda i, dy: gram_ref[i, HALO + dy : HALO + dy + 8], 1.0 / (members - 1))

    slot, turned = turning(8)

    def one_probe(p, _):
        start = TOP + HALO
        b = weighted(weight_ref, [prob_ref[p, start + dy : start + dy + 8] for dy in range(-HALO, HALO + 1)])
        mid_ref[p] = turned(b, HALO - 3 * STRIP)
        rest = jnp.where(slot < STRIP, turned(b, WIN + HALO), turned(b, 2 * WIN + HALO - STRIP))
        rest = jnp.where(slot < 2 * STRIP, rest, pltpu.roll(lanes_by(rest, 2 * STRIP), HALO, 0))
        out_ref[p, 2] = rest[:HALO]
        return 0

    lax.fori_loop(0, members, one_probe, 0, unroll=16)


def apply_kernel(
    n_row, rates_ref, ends_ref, cls_ref, below_ref, above_ref, own_ref, mid_ref, part_ref, third_ref, out_ref,
    prob_ref, gram_ref, weight_ref, rate_ref,
):
    members = ends_ref.shape[0]
    has_below = lax.axis_index("row") != n_row - 1
    has_above = lax.axis_index("row") != 0
    blank = jnp.zeros((HALO, LANES), F32)
    sub = lax.broadcasted_iota(jnp.int32, (8, LANES), 0)
    upper = sub < HALO
    crossing = [d for d in FORWARD if d[0] > 0]

    def spread(m, acc):
        ends = ends_ref[m]
        below, above = below_ref[m].astype(F32), above_ref[m].astype(F32)
        prob_ref[m, TOP - HALO : TOP] = above[HALO:]
        prob_ref[m, TOP + ROWS : TOP + ROWS + HALO] = below[HALO:]
        low = jnp.where(upper, ends, pltpu.roll(below, HALO, 0))
        high = jnp.where(upper, above, ends)
        high = {dy: pltpu.roll(high, HALO + dy, 0) if dy < HALO else high for dy in range(1, HALO + 1)}
        near = {dx: lanes_by(low, dx) for dx in range(-HALO + 1, HALO)}
        return tuple(a + high[dy] * near[dx] for a, (dy, dx) in zip(acc, crossing))

    acc = tuple(jnp.zeros((8, LANES), F32) for _ in crossing)
    acc = lax.fori_loop(0, members, spread, acc, unroll=4)
    inside = (upper & has_above) | (jnp.logical_not(upper) & has_below)
    acc = {d: jnp.where(inside, a, 0.0) for d, a in zip(crossing, acc)}
    for i, d in enumerate(FORWARD):
        gram_ref[i, 8:16] = own_ref[i, 8:16]
        if d in acc:
            gram_ref[i, 0:8] = own_ref[i, 0:8] + jnp.where(sub < d[0], acc[d], 0.0)
            gram_ref[i, 16:24] = pltpu.roll(acc[d], HALO, 0)
        else:
            gram_ref[i, 0:8] = own_ref[i, 0:8]

    cls = jnp.concatenate(
        [
            blank,
            jnp.where(has_above, above_ref[members, :HALO].astype(F32), 0.0),
            cls_ref[...],
            jnp.where(has_below, below_ref[members, :HALO].astype(F32), 0.0),
            blank,
        ],
        axis=0,
    )
    rate_ref[...] = rates_of(cls, rates_ref)
    coef = entries(
        lambda dy: jnp.where(upper, rate_ref[TOP + dy : TOP + dy + 8], rate_ref[TOP + 8 + dy : TOP + dy + 16])
    )
    set_weights(
        weight_ref,
        coef,
        lambda i, dy: jnp.where(upper, gram_ref[i, dy : dy + 8], gram_ref[i, 8 + dy : dy + 16]),
        1.0 / (members - 1),
    )

    slot, turned = turning(8)

    def some_probes(i, _):
        some = [2 * i + j for j in range(2)]
        rows = [
            [
                jnp.where(upper, prob_ref[p, TOP + dy : TOP + dy + 8], prob_ref[p, TOP + 8 + dy : TOP + dy + 16])
                for dy in range(-HALO, HALO + 1)
            ]
            for p in some
        ]
        total = [None for p in some]
        for dx in range(-HALO, HALO + 1):
            part = [None for p in some]
            for dy in range(-HALO + abs(dx), HALO - abs(dx) + 1):
                weight = weight_ref[AT[(dy, dx)]]
                for j in range(2):
                    term = weight * rows[j][dy + HALO]
                    part[j] = term if part[j] is None else part[j] + term
            for j in range(2):
                moved = lanes_by(part[j], dx)
                total[j] = moved if total[j] is None else total[j] + moved
        for p, a in zip(some, total):
            first = jnp.where(slot < STRIP, turned(a, HALO), turned(a, HALO + 8))
            first = jnp.where(slot < 2 * STRIP, first, turned(a, HALO + 16))
            first = jnp.where(slot < 3 * STRIP, first, mid_ref[p])
            out_ref[p, 0] = first[:HALO]
            out_ref[p, 1] = first[HALO:]
        return 0

    lax.fori_loop(0, members // 2, some_probes, 0, unroll=8)


def unpack_kernel(got_ref, out_ref, tile_ref, sems):
    per = LANES // STRIP
    blocks = COLS // LANES
    slots = [lax.broadcasted_iota(jnp.int32, (rows, LANES), 1) // STRIP for rows in (HALO, 8)]

    def joined(parts, first):
        slot = slots[0] if parts[0].shape[0] == HALO else slots[1]
        acc = parts[0]
        for q in range(1, per):
            acc = jnp.where(slot == (first + q) % per, parts[q], acc)
        return pltpu.roll(acc, (-first * STRIP) % LANES, 1) if first % per else acc

    copies = []
    for l in range(LEV):
        for at in range(blocks):
            got = [got_ref[(at * per + q) * LEV + l] for q in range(per)]
            top = [jnp.concatenate([g[0], g[1]], axis=0) for g in got]
            low = [g[2] for g in got]
            span = slice(at * LANES, (at + 1) * LANES)
            for v in range(VARS):
                ends = joined(top, v)
                tile_ref[v, l, :HALO, span] = ends[:HALO]
                tile_ref[v, l, ROWS - HALO :, span] = ends[HALO:]
                if v == 0:
                    tile_ref[v, l, HALO : HALO + 8, span] = joined(top, VARS)
                else:
                    tile_ref[v, l, HALO : 2 * HALO, span] = joined(low, v - 1)
                    tile_ref[v, l, 2 * HALO : 3 * HALO, span] = joined(low, v + 1)
        for v in range(VARS):
            copy = pltpu.make_async_copy(tile_ref.at[v, l], out_ref.at[0, v, l], sems.at[v * LEV + l])
            copy.start()
            copies.append(copy)
    for copy in copies:
        copy.wait()


def body(pert, probes, diff_class, class_rate):
    members = lax.axis_size("member")
    n_row = lax.axis_size("row")
    vmem = pl.BlockSpec(memory_space=pltpu.VMEM)
    smem = pl.BlockSpec(memory_space=pltpu.SMEM)
    shape = pltpu.VMEM

    def near(x):
        return pltpu.with_memory_space_constraint(x, pltpu.VMEM)

    end = pltpu.VMEM((VARS, LEV, ROWS, LANES), BF16)
    side = pl.pallas_call(
        side_kernel,
        in_specs=[pl.BlockSpec(memory_space=pl.ANY)] * 3,
        out_specs=vmem,
        out_shape=shape(((2 * LEV + 1) * ROWS, LANES), BF16),
        scratch_shapes=[end, end, pltpu.VMEM((ROWS, LANES), jnp.int32), pltpu.SemaphoreType.DMA((3,))],
        name="side",
    )(pert, probes, diff_class)
    beside = lax.ppermute(side, "col", [(0, 1), (1, 0)])

    chunk, classes = shape((members, 2 * ROWS, LANES), BF16), shape((ROWS, LANES), F32)
    inner, cls, rates = pl.pallas_call(
        pack_kernel,
        in_specs=[smem] + [vmem] * 3,
        out_specs=[vmem] * 3,
        out_shape=[chunk, classes, shape((class_rate.shape[0], LANES), F32)],
        scratch_shapes=[pltpu.VMEM((ROWS, COLS + 2 * LANES), BF16)],
        name="pack",
    )(class_rate, pert, probes, diff_class)
    chunks, cls = pl.pallas_call(
        patch_kernel,
        in_specs=[vmem] * 3,
        out_specs=[vmem] * 2,
        out_shape=[chunk, classes],
        input_output_aliases={1: 0},
        name="patch",
    )(near(beside), near(inner), near(cls))

    got = lax.all_to_all(chunks, "member", 0, 0, tiled=True)

    edge = shape((members + 1, 8, LANES), BF16)
    up, dn = pl.pallas_call(
        edge_kernel,
        in_specs=[vmem] * 2,
        out_specs=[vmem] * 2,
        out_shape=[edge, edge],
        name="edges",
    )(near(got), near(cls))
    below = lax.ppermute(up, "row", [(i, (i - 1) % n_row) for i in range(n_row)])
    above = lax.ppermute(dn, "row", [(i, (i + 1) % n_row) for i in range(n_row)])

    tall = shape((members, TALL, LANES), F32)
    weights = pltpu.VMEM((len(EVERY), 8, LANES), F32)
    third = shape((members, VARS, HALO, LANES), F32)
    eight = shape((members, 8, LANES), F32)
    own, spread, mid, part, ends = pl.pallas_call(
        own_kernel,
        in_specs=[vmem] * 3,
        out_specs=[vmem] * 5,
        out_shape=[shape((len(FORWARD), ROWS, LANES), F32), tall, eight, third, eight],
        scratch_shapes=[
            pltpu.VMEM((members, TOP + ROWS, LANES), F32),
            weights,
            pltpu.VMEM((ROWS, LANES), F32),
        ],
        name="own",
    )(near(rates), near(got), near(cls))

    part, spread = pl.pallas_call(
        functools.partial(apply_kernel, n_row),
        in_specs=[vmem] * 9,
        out_specs=[vmem] * 2,
        out_shape=[third, tall],
        input_output_aliases={7: 1, 8: 0},
        scratch_shapes=[
            pltpu.VMEM((len(FORWARD), 24, LANES), F32),
            weights,
            pltpu.VMEM((TALL, LANES), F32),
        ],
        name="apply",
    )(near(rates), near(ends), near(cls), near(below), near(above), near(own), near(mid), near(spread), near(part))

    back = lax.all_to_all(part, "member", 0, 0, tiled=True)

    return pl.pallas_call(
        unpack_kernel,
        in_specs=[vmem],
        out_specs=pl.BlockSpec(memory_space=pl.ANY),
        out_shape=jax.ShapeDtypeStruct((1, VARS, LEV, ROWS, COLS), F32),
        scratch_shapes=[
            pltpu.VMEM((VARS, LEV, ROWS, COLS), F32),
            pltpu.SemaphoreType.DMA((VARS * LEV,)),
        ],
        name="unpack",
    )(near(back))


def solution(mesh):
    placed = (
        P("member", None, None, "row", "col"),
        P("member", None, None, "row", "col"),
        P("row", "col"),
        P(),
    )
    return jax.shard_map(
        body,
        mesh=mesh,
        in_specs=placed,
        out_specs=P("member", None, None, "row", "col"),
        check_vma=False,
    )
```

```python
import functools

import jax
import jax.numpy as jnp
from jax import lax
from jax.experimental import pallas as pl
from jax.experimental.pallas import tpu as pltpu
from jax.sharding import PartitionSpec as P

SWEEPS = 4
VARS = 3
LEV = 2
ROWS = 16
COLS = 512
HALO = 4
STRIP = 32
WIN = STRIP + 2 * HALO
LANES = 128
F32 = jnp.float32
BF16 = jnp.bfloat16


def grouped(a, b):
    upper = lax.broadcasted_iota(jnp.int32, (8, LANES), 0) < HALO
    groups = [
        jnp.where(upper, a[:8], pltpu.roll(b[:8], HALO, 0)),
        jnp.where(upper, pltpu.roll(a[8:], HALO, 0), b[8:]),
        jnp.where(upper, pltpu.roll(a[:8], HALO, 0), b[:8]),
        jnp.where(upper, a[8:], pltpu.roll(b[8:], HALO, 0)),
    ]
    return jnp.concatenate(groups, axis=0).astype(BF16)


def side_kernel(pert_ref, prob_ref, cls_ref, side_ref, pert_end, prob_end, cls_end, sems):
    last = lax.axis_index("col") == 0
    at = pl.ds(pl.multiple_of(jnp.where(last, COLS - LANES, 0), LANES), LANES)
    copies = [
        pltpu.make_async_copy(pert_ref.at[0, :, :, :, at], pert_end, sems.at[0]),
        pltpu.make_async_copy(prob_ref.at[0, :, :, :, at], prob_end, sems.at[1]),
        pltpu.make_async_copy(cls_ref.at[:, at], cls_end, sems.at[2]),
    ]
    for copy in copies:
        copy.start()
    lane = lax.broadcasted_iota(jnp.int32, (ROWS, LANES), 1)
    low = jnp.where(last, 0, WIN - HALO)
    use = [(lane >= WIN * v + low) & (lane < WIN * v + low + HALO) for v in range(VARS)]
    for copy in copies:
        copy.wait()

    def placed(planes):
        acc = jnp.zeros((ROWS, LANES), F32)
        for v, plane in enumerate(planes):
            shift = jnp.where(last, WIN * v + HALO, WIN * v + WIN - HALO)
            acc = jnp.where(use[v], pltpu.roll(plane, shift, 1), acc)
        return acc

    for l in range(LEV):
        a, b = (placed([end[v, l].astype(F32) for v in range(VARS)]) for end in (pert_end, prob_end))
        side_ref[l * 2 * ROWS : (l + 1) * 2 * ROWS] = grouped(a, b)
    side_ref[LEV * 2 * ROWS :] = placed([(cls_end[...] + 1).astype(F32)] * VARS).astype(BF16)


def pack_kernel(rates_ref, pert_ref, prob_ref, cls_ref, out_ref, cls_out_ref, rates_out_ref, wide_ref):
    lane = lax.broadcasted_iota(jnp.int32, (ROWS, LANES), 1)
    blocks = COLS // LANES
    for k in range(rates_ref.shape[0]):
        rates_out_ref[k : k + 1] = jnp.full((1, LANES), rates_ref[k], F32)

    def block(ref, v, l, at, shift):
        got = ref[0, v, l, :, at * LANES : (at + 1) * LANES].astype(F32)
        return pltpu.roll(got, shift, 1) if shift else got

    for s in range(COLS // STRIP):
        start = s * STRIP - HALO
        at, off = start // LANES, start % LANES
        for l in range(LEV):
            both = []
            for ref in (pert_ref, prob_ref):
                acc = jnp.zeros((ROWS, LANES), F32)
                for v in range(VARS):
                    shift = (WIN * v - off) % LANES
                    low, high = WIN * v, WIN * (v + 1)
                    split = low + LANES - off
                    if at >= 0:
                        use = (lane >= low) & (lane < min(high, split))
                        acc = jnp.where(use, block(ref, v, l, at, shift), acc)
                    if split < high and at + 1 < blocks:
                        use = (lane >= split) & (lane < high)
                        acc = jnp.where(use, block(ref, v, l, at + 1, shift), acc)
                both.append(acc)
            out_ref[s * LEV + l] = grouped(*both)

    zero = jnp.zeros((ROWS, LANES), BF16)
    wide_ref[:, :LANES] = zero
    wide_ref[:, LANES : LANES + COLS] = (cls_ref[...] + 1).astype(F32).astype(BF16)
    wide_ref[:, LANES + COLS :] = zero
    strip = lax.axis_index("member") // LEV
    wide = wide_ref.shape[1]
    spot = lax.broadcasted_iota(jnp.int32, (wide, LANES), 0)
    lane = lax.broadcasted_iota(jnp.int32, (wide, LANES), 1)
    column = lane - jnp.where(lane >= WIN, WIN, 0) - jnp.where(lane >= 2 * WIN, WIN, 0)
    pick = (spot == LANES - HALO + STRIP * strip + column) & (lane < VARS * WIN)
    cls_out_ref[...] = jnp.dot(wide_ref[...], pick.astype(F32).astype(BF16), preferred_element_type=F32)


def patch_kernel(side_ref, inner_ref, cls_ref, out_ref, cls_out_ref):
    first = lax.axis_index("col") == 0
    strip = lax.axis_index("member") // LEV
    end = COLS // STRIP - 1
    for l in range(LEV):
        side = side_ref[l * 2 * ROWS : (l + 1) * 2 * ROWS].astype(F32)
        for s, here in ((0, jnp.logical_not(first)), (end, first)):
            at = s * LEV + l
            out_ref[at] = (inner_ref[at].astype(F32) + jnp.where(here, side, 0.0)).astype(BF16)
    mine = strip == jnp.where(first, end, 0)
    cls_out_ref[...] = cls_ref[...] + jnp.where(mine, side_ref[LEV * 2 * ROWS :].astype(F32), 0.0)


def edge_kernel(got_ref, cls_ref, up_ref, dn_ref):
    members = got_ref.shape[0]
    up_ref[:members] = got_ref[:, :8]
    dn_ref[:members] = got_ref[:, 8:16]
    up_ref[members] = cls_ref[:8].astype(BF16)
    dn_ref[members] = pltpu.roll(cls_ref[8:], HALO, 0).astype(BF16)


TOP = 8
TALL = TOP + ROWS + TOP
FORWARD = [
    (dy, dx)
    for dy in range(HALO + 1)
    for dx in range(-HALO, HALO + 1)
    if dy + abs(dx) <= HALO and (dy > 0 or dx >= 0)
]
EVERY = [(dy, dx) for dx in range(-HALO, HALO + 1) for dy in range(-HALO, HALO + 1) if abs(dy) + abs(dx) <= HALO]
AT = {d: i for i, d in enumerate(EVERY)}


def lanes_by(x, dx):
    return pltpu.roll(x, (-dx) % LANES, 1) if dx else x


def rates_of(cls, rates_ref):
    rate = jnp.zeros(cls.shape, F32)
    for k in range(rates_ref.shape[0]):
        rate = jnp.where(cls == float(k + 1), rates_ref[k : k + 1], rate)
    return rate


def entries(rows_at):
    steps = ((0, 1), (0, -1), (1, 0), (-1, 0))
    near = {dy: rows_at(dy) for dy in range(-HALO + 1, HALO)}
    at = {(dy, dx): lanes_by(near[dy], dx) for dy, dx in EVERY if abs(dy) + abs(dx) < HALO}
    coef = {(0, 0): 1.0 - 4.0 * at[(0, 0)]}
    for e in steps:
        coef[e] = at[(0, 0)]
    for sweep in range(1, SWEEPS):
        flow = {d: c * at[d] for d, c in coef.items()}
        to = {(d[0] + e[0], d[1] + e[1]) for d in flow for e in steps}
        new = {}
        for d in EVERY:
            if d not in to:
                continue
            terms = [flow[(d[0] - e[0], d[1] - e[1])] for e in steps if (d[0] - e[0], d[1] - e[1]) in flow]
            if d in coef:
                terms.append(coef[d] - 4.0 * flow[d])
            total = terms[0]
            for t in terms[1:]:
                total = total + t
            new[d] = total
        coef = new
    return coef


def set_weights(weight_ref, coef, gram_at, scale):
    for i, (dy, dx) in enumerate(FORWARD):
        weight_ref[AT[(dy, dx)]] = lanes_by(coef[(dy, dx)] * scale * gram_at(i, dy), -dx)
        if (dy, dx) != (0, 0):
            weight_ref[AT[(-dy, -dx)]] = lanes_by(coef[(-dy, -dx)] * scale, dx) * gram_at(i, 0)


def weighted(weight_ref, rows):
    total = None
    for dx in range(-HALO, HALO + 1):
        part = None
        for dy in range(-HALO + abs(dx), HALO - abs(dx) + 1):
            term = weight_ref[AT[(dy, dx)]] * rows[dy + HALO]
            part = term if part is None else part + term
        part = lanes_by(part, dx)
        total = part if total is None else total + part
    return total


def turning(rows):
    turn = lax.axis_index("member") // LEV % (LANES // STRIP) * STRIP
    slot = (lax.broadcasted_iota(jnp.int32, (rows, LANES), 1) - turn) & (LANES - 1)

    def turned(x, dx):
        return pltpu.roll(x, (turn + (-dx) % LANES) & (LANES - 1), 1)

    return slot, turned


def own_kernel(rates_ref, got_ref, cls_ref, gram_ref, prob_ref, mid_ref, out_ref, pert_ref, weight_ref, rate_ref):
    members = got_ref.shape[0]
    blank = jnp.zeros((TOP, LANES), F32)

    def spread(m, _):
        tile = got_ref[m].astype(F32)
        pert_ref[m, 0:TOP] = blank
        for group, to in enumerate((0, 12, 4, 8)):
            pert_ref[m, TOP + to : TOP + to + HALO] = tile[8 * group : 8 * group + HALO]
            prob_ref[m, TOP + to : TOP + to + HALO] = tile[8 * group + HALO : 8 * group + 8]
        return 0

    lax.fori_loop(0, members, spread, 0, unroll=4)
    for b in range(2):
        row = TOP + 8 * b

        def products(m, acc):
            low = pert_ref[m, row : row + 8]
            high = [pert_ref[m, row - dy : row - dy + 8] for dy in range(HALO + 1)]
            near = {dx: lanes_by(low, dx) for dx in range(-HALO + 1, HALO + 1)}
            return tuple(a + high[dy] * near[dx] for a, (dy, dx) in zip(acc, FORWARD))

        acc = tuple(jnp.zeros((8, LANES), F32) for _ in FORWARD)
        acc = lax.fori_loop(0, members, products, acc, unroll=16)
        for i, a in enumerate(acc):
            gram_ref[i, 8 * b : 8 * b + 8] = a

    rate_ref[...] = rates_of(cls_ref[...], rates_ref)
    coef = entries(lambda dy: rate_ref[HALO + dy : HALO + dy + 8])
    set_weights(weight_ref, coef, lambda i, dy: gram_ref[i, HALO + dy : HALO + dy + 8], 1.0 / (members - 1))

    slot, turned = turning(8)

    def one_probe(p, _):
        start = TOP + HALO
        b = weighted(weight_ref, [prob_ref[p, start + dy : start + dy + 8] for dy in range(-HALO, HALO + 1)])
        mid_ref[p] = turned(b, HALO - 3 * STRIP)
        rest = jnp.where(slot < STRIP, turned(b, WIN + HALO), turned(b, 2 * WIN + HALO - STRIP))
        rest = jnp.where(slot < 2 * STRIP, rest, pltpu.roll(lanes_by(rest, 2 * STRIP), HALO, 0))
        out_ref[p, 2] = rest[:HALO]
        return 0

    lax.fori_loop(0, members, one_probe, 0, unroll=16)


def apply_kernel(
    n_row, rates_ref, got_ref, cls_ref, below_ref, above_ref, own_ref, mid_ref, part_ref, third_ref, out_ref,
    prob_ref, gram_ref, weight_ref, rate_ref,
):
    members = got_ref.shape[0]
    has_below = lax.axis_index("row") != n_row - 1
    has_above = lax.axis_index("row") != 0
    blank = jnp.zeros((HALO, LANES), F32)
    sub = lax.broadcasted_iota(jnp.int32, (8, LANES), 0)
    upper = sub < HALO
    crossing = [d for d in FORWARD if d[0] > 0]

    def spread(m, acc):
        tile = got_ref[m, :ROWS].astype(F32)
        below, above = below_ref[m].astype(F32), above_ref[m].astype(F32)
        prob_ref[m, TOP - HALO : TOP] = above[HALO:]
        prob_ref[m, TOP + ROWS : TOP + ROWS + HALO] = below[HALO:]
        low = jnp.where(upper, tile[0:8], pltpu.roll(below, HALO, 0))
        high = jnp.where(upper, above, pltpu.roll(tile[8:16], HALO, 0))
        high = {dy: pltpu.roll(high, HALO + dy, 0) if dy < HALO else high for dy in range(1, HALO + 1)}
        near = {dx: lanes_by(low, dx) for dx in range(-HALO + 1, HALO)}
        return tuple(a + high[dy] * near[dx] for a, (dy, dx) in zip(acc, crossing))

    acc = tuple(jnp.zeros((8, LANES), F32) for _ in crossing)
    acc = lax.fori_loop(0, members, spread, acc, unroll=4)
    inside = (upper & has_above) | (jnp.logical_not(upper) & has_below)
    acc = {d: jnp.where(inside, a, 0.0) for d, a in zip(crossing, acc)}
    for i, d in enumerate(FORWARD):
        gram_ref[i, 8:16] = own_ref[i, 8:16]
        if d in acc:
            gram_ref[i, 0:8] = own_ref[i, 0:8] + jnp.where(sub < d[0], acc[d], 0.0)
            gram_ref[i, 16:24] = pltpu.roll(acc[d], HALO, 0)
        else:
            gram_ref[i, 0:8] = own_ref[i, 0:8]

    cls = jnp.concatenate(
        [
            blank,
            jnp.where(has_above, above_ref[members, :HALO].astype(F32), 0.0),
            cls_ref[...],
            jnp.where(has_below, below_ref[members, :HALO].astype(F32), 0.0),
            blank,
        ],
        axis=0,
    )
    rate_ref[...] = rates_of(cls, rates_ref)
    coef = entries(
        lambda dy: jnp.where(upper, rate_ref[TOP + dy : TOP + dy + 8], rate_ref[TOP + 8 + dy : TOP + dy + 16])
    )
    set_weights(
        weight_ref,
        coef,
        lambda i, dy: jnp.where(upper, gram_ref[i, dy : dy + 8], gram_ref[i, 8 + dy : dy + 16]),
        1.0 / (members - 1),
    )

    slot, turned = turning(8)

    def some_probes(i, _):
        some = [2 * i + j for j in range(2)]
        rows = [
            [
                jnp.where(upper, prob_ref[p, TOP + dy : TOP + dy + 8], prob_ref[p, TOP + 8 + dy : TOP + dy + 16])
                for dy in range(-HALO, HALO + 1)
            ]
            for p in some
        ]
        total = [None for p in some]
        for dx in range(-HALO, HALO + 1):
            part = [None for p in some]
            for dy in range(-HALO + abs(dx), HALO - abs(dx) + 1):
                weight = weight_ref[AT[(dy, dx)]]
                for j in range(2):
                    term = weight * rows[j][dy + HALO]
                    part[j] = term if part[j] is None else part[j] + term
            for j in range(2):
                moved = lanes_by(part[j], dx)
                total[j] = moved if total[j] is None else total[j] + moved
        for p, a in zip(some, total):
            first = jnp.where(slot < STRIP, turned(a, HALO), turned(a, HALO + 8))
            first = jnp.where(slot < 2 * STRIP, first, turned(a, HALO + 16))
            first = jnp.where(slot < 3 * STRIP, first, mid_ref[p])
            out_ref[p, 0] = first[:HALO]
            out_ref[p, 1] = first[HALO:]
        return 0

    lax.fori_loop(0, members // 2, some_probes, 0, unroll=8)


def unpack_kernel(got_ref, out_ref, tile_ref, sems):
    per = LANES // STRIP
    blocks = COLS // LANES
    slots = [lax.broadcasted_iota(jnp.int32, (rows, LANES), 1) // STRIP for rows in (HALO, 8)]

    def joined(parts, first):
        slot = slots[0] if parts[0].shape[0] == HALO else slots[1]
        acc = parts[0]
        for q in range(1, per):
            acc = jnp.where(slot == (first + q) % per, parts[q], acc)
        return pltpu.roll(acc, (-first * STRIP) % LANES, 1) if first % per else acc

    copies = []
    for l in range(LEV):
        for at in range(blocks):
            got = [got_ref[(at * per + q) * LEV + l] for q in range(per)]
            top = [jnp.concatenate([g[0], g[1]], axis=0) for g in got]
            low = [g[2] for g in got]
            span = slice(at * LANES, (at + 1) * LANES)
            for v in range(VARS):
                ends = joined(top, v)
                tile_ref[v, l, :HALO, span] = ends[:HALO]
                tile_ref[v, l, ROWS - HALO :, span] = ends[HALO:]
                if v == 0:
                    tile_ref[v, l, HALO : HALO + 8, span] = joined(top, VARS)
                else:
                    tile_ref[v, l, HALO : 2 * HALO, span] = joined(low, v - 1)
                    tile_ref[v, l, 2 * HALO : 3 * HALO, span] = joined(low, v + 1)
        for v in range(VARS):
            copy = pltpu.make_async_copy(tile_ref.at[v, l], out_ref.at[0, v, l], sems.at[v * LEV + l])
            copy.start()
            copies.append(copy)
    for copy in copies:
        copy.wait()


def body(pert, probes, diff_class, class_rate):
    members = lax.axis_size("member")
    n_row = lax.axis_size("row")
    vmem = pl.BlockSpec(memory_space=pltpu.VMEM)
    smem = pl.BlockSpec(memory_space=pltpu.SMEM)
    shape = pltpu.VMEM

    def near(x):
        return pltpu.with_memory_space_constraint(x, pltpu.VMEM)

    end = pltpu.VMEM((VARS, LEV, ROWS, LANES), BF16)
    side = pl.pallas_call(
        side_kernel,
        in_specs=[pl.BlockSpec(memory_space=pl.ANY)] * 3,
        out_specs=vmem,
        out_shape=shape(((2 * LEV + 1) * ROWS, LANES), BF16),
        scratch_shapes=[end, end, pltpu.VMEM((ROWS, LANES), jnp.int32), pltpu.SemaphoreType.DMA((3,))],
        name="side",
    )(pert, probes, diff_class)
    beside = lax.ppermute(side, "col", [(0, 1), (1, 0)])

    chunk, classes = shape((members, 2 * ROWS, LANES), BF16), shape((ROWS, LANES), F32)
    inner, cls, rates = pl.pallas_call(
        pack_kernel,
        in_specs=[smem] + [vmem] * 3,
        out_specs=[vmem] * 3,
        out_shape=[chunk, classes, shape((class_rate.shape[0], LANES), F32)],
        scratch_shapes=[pltpu.VMEM((ROWS, COLS + 2 * LANES), BF16)],
        name="pack",
    )(class_rate, pert, probes, diff_class)
    chunks, cls = pl.pallas_call(
        patch_kernel,
        in_specs=[vmem] * 3,
        out_specs=[vmem] * 2,
        out_shape=[chunk, classes],
        input_output_aliases={1: 0},
        name="patch",
    )(near(beside), near(inner), near(cls))

    got = lax.all_to_all(chunks, "member", 0, 0, tiled=True)

    edge = shape((members + 1, 8, LANES), BF16)
    up, dn = pl.pallas_call(
        edge_kernel,
        in_specs=[vmem] * 2,
        out_specs=[vmem] * 2,
        out_shape=[edge, edge],
        name="edges",
    )(near(got), near(cls))
    below = lax.ppermute(up, "row", [(i, (i - 1) % n_row) for i in range(n_row)])
    above = lax.ppermute(dn, "row", [(i, (i + 1) % n_row) for i in range(n_row)])

    tall = shape((members, TALL, LANES), F32)
    weights = pltpu.VMEM((len(EVERY), 8, LANES), F32)
    third = shape((members, VARS, HALO, LANES), F32)
    own, spread, mid, part = pl.pallas_call(
        own_kernel,
        in_specs=[vmem] * 3,
        out_specs=[vmem] * 4,
        out_shape=[shape((len(FORWARD), ROWS, LANES), F32), tall, shape((members, 8, LANES), F32), third],
        scratch_shapes=[
            pltpu.VMEM((members, TOP + ROWS, LANES), F32),
            weights,
            pltpu.VMEM((ROWS, LANES), F32),
        ],
        name="own",
    )(near(rates), near(got), near(cls))

    part, spread = pl.pallas_call(
        functools.partial(apply_kernel, n_row),
        in_specs=[vmem] * 9,
        out_specs=[vmem] * 2,
        out_shape=[third, tall],
        input_output_aliases={7: 1, 8: 0},
        scratch_shapes=[
            pltpu.VMEM((len(FORWARD), 24, LANES), F32),
            weights,
            pltpu.VMEM((TALL, LANES), F32),
        ],
        name="apply",
    )(near(rates), near(got), near(cls), near(below), near(above), near(own), near(mid), near(spread), near(part))

    back = lax.all_to_all(part, "member", 0, 0, tiled=True)

    return pl.pallas_call(
        unpack_kernel,
        in_specs=[vmem],
        out_specs=pl.BlockSpec(memory_space=pl.ANY),
        out_shape=jax.ShapeDtypeStruct((1, VARS, LEV, ROWS, COLS), F32),
        scratch_shapes=[
            pltpu.VMEM((VARS, LEV, ROWS, COLS), F32),
            pltpu.SemaphoreType.DMA((VARS * LEV,)),
        ],
        name="unpack",
    )(near(back))


def solution(mesh):
    placed = (
        P("member", None, None, "row", "col"),
        P("member", None, None, "row", "col"),
        P("row", "col"),
        P(),
    )
    return jax.shard_map(
        body,
        mesh=mesh,
        in_specs=placed,
        out_specs=P("member", None, None, "row", "col"),
        check_vma=False,
    )
```
